32 devices in a mesh: dp: 8 (over y, x, core), mp: 4 (over z).
Axes of the slice: x: 2, y: 2, z: 4, core: 2. Of those that a mesh axis runs over, the one named last changes fastest.
Arguments:
- stream: float32 [16384, 768], P('dp', 'mp'), may hold values from -6 to 6
- seq_lens: int32 [32], P('dp'), may hold values from 0 to 2048, as said below
- w_qkv: bfloat16 [2, 768, 3, 768], P(None, None, None, 'mp'), may hold values from -0.3125 to 0.3125
- b_qv: float32 [2, 2, 768], P(None, None, 'mp'), may hold values from -3 to 3
- w_out: bfloat16 [2, 768, 768], P(None, 'mp'), may hold values from -0.625 to 0.625
- b_out: float32 [2, 768], P(None, 'mp'), may hold values from -2 to 2
- w_up: bfloat16 [2, 768, 3072], P(None, None, 'mp'), may hold values from -0.21875 to 0.21875
- b_up: float32 [2, 3072], P(None, 'mp'), may hold values from -3 to 3
- w_down: bfloat16 [2, 3072, 768], P(None, 'mp'), may hold values from -0.15625 to 0.15625
- b_down: float32 [2, 768], P(None, 'mp'), may hold values from -2 to 2
- cotangent: float32 [16384, 768], P('dp', 'mp'), may hold values from -6 to 6
Outputs:
- out_first: float32 [16384, 768], P('dp', 'mp')
- out_second: float32 [16384, 768], P('dp', 'mp')
- grad_stream: float32 [16384, 768], P('dp', 'mp')
- grad_w_qkv: float32 [2, 768, 3, 768], P(None, None, None, 'mp')
- grad_b_qv: float32 [2, 2, 768], P(None, None, 'mp')
- grad_w_out: float32 [2, 768, 768], P(None, 'mp')
- grad_b_out: float32 [2, 768], P(None, 'mp')
- grad_w_up: float32 [2, 768, 3072], P(None, None, 'mp')
- grad_b_up: float32 [2, 3072], P(None, 'mp')
- grad_w_down: float32 [2, 3072, 768], P(None, 'mp')
- grad_b_down: float32 [2, 768], P(None, 'mp')
The draws below stay inside these ranges and needn't reach their ends.
Inputs may be any that keep to these rules, and one draw needn't show every extreme that they name: `seq_lens`: each index of dp holds 2048 tokens in its 4 entries: either one sequence of 2048 tokens followed by zeros, or 4 sequences of 512 tokens; exactly half of the indices hold the single sequence, which ones is drawn from the seed.
All inputs are finite; a program needn't handle non-finite values.
Results may differ from the reference program's by a relative error of at most 0.029.
Values may be sent and summed in bfloat16 or wider, within the bound.
No kernel may reach another device: no remote copies, remote signals or barrier semaphores. Data moves between devices by JAX's collectives and lax.ppermute only.
A program may use at most 256 MiB of HBM per device.

```python
import jax
import jax.numpy as jnp
from jax import lax

D = 768
HEADS = 12
FF = 3072
LAYERS = 2
SHORT = 512
TOK_DEV = 2048
SLOTS = 4
NSEQ = 32
TOKENS = 16384


def draw_seq_lens(key, part):
    groups = NSEQ // SLOTS
    order = jax.random.permutation(key, groups)
    longer = order < groups // 2
    slot_ids = jnp.arange(SLOTS, dtype=jnp.int32)
    long_row = jnp.where(slot_ids == 0, TOK_DEV, 0).astype(jnp.int32)
    short_row = jnp.full((SLOTS,), SHORT, jnp.int32)
    table = jnp.where(longer[:, None], long_row[None, :], short_row[None, :])
    return table.reshape(NSEQ).astype(jnp.int32)


def steps_of(own_key, shape, cuts, low, top_value):
    factor_of = 1.0
    for position, shards_of in cuts:
        steps = jax.random.uniform(jax.random.fold_in(jax.random.fold_in(own_key, 6), position), (shards_of,), jnp.float32, low / len(cuts), top_value / len(cuts))
        factor_of = factor_of * jnp.repeat(jnp.exp(steps), shape[position] // shards_of).reshape((-1,) + (1,) * (len(shape) - 1 - position))
    return factor_of


def scatter_about(stream_key, extent, scale, limit, pieces=(), kind=jnp.bfloat16):
    drawn = jax.random.normal(stream_key, extent, jnp.float32) * scale
    if len(pieces) > 0:
        drawn = steps_of(stream_key, extent, pieces, -0.22, 0.18) * drawn
    return jnp.clip(drawn, min=-limit, max=limit).astype(kind)


def setup_inputs(seed: int = 0) -> dict:
    arg_keys = jax.random.split(jax.random.key(seed), 12)
    return {
        "stream": scatter_about(arg_keys[0], (TOKENS, D), 1.0, 6.0, ((0, 8), (1, 4)), jnp.float32),
        "seq_lens": draw_seq_lens(jax.random.fold_in(arg_keys[11], 71), 0),
        "w_qkv": scatter_about(arg_keys[2], (LAYERS, D, 3, D), (D // 2) ** -0.5, 0.3125, ((3, 4),)),
        "b_qv": scatter_about(arg_keys[3], (LAYERS, 2, D), 0.5, 3.0, ((2, 4),), jnp.float32),
        "w_out": scatter_about(arg_keys[4], (LAYERS, D, D), (D // 8) ** -0.5, 0.625, ((1, 4),)),
        "b_out": scatter_about(arg_keys[5], (LAYERS, D), 0.3, 2.0, ((1, 4),), jnp.float32),
        "w_up": scatter_about(arg_keys[6], (LAYERS, D, FF), D ** -0.5, 0.21875, ((2, 4),)),
        "b_up": scatter_about(arg_keys[7], (LAYERS, FF), 0.5, 3.0, ((1, 4),), jnp.float32),
        "w_down": scatter_about(arg_keys[8], (LAYERS, FF, D), (FF // 2) ** -0.5, 0.15625, ((1, 4),)),
        "b_down": scatter_about(arg_keys[9], (LAYERS, D), 0.3, 2.0, ((1, 4),), jnp.float32),
        "cotangent": scatter_about(arg_keys[10], (TOKENS, D), 1.0, 6.0, ((0, 8), (1, 4)), jnp.float32),
    }


EPS = 1e-06
HIGH = lax.Precision.HIGHEST

@jax.custom_vjp
def low(v):
    return lax.optimization_barrier(v.astype(jnp.bfloat16)).astype(jnp.float32)

@jax.custom_vjp
def low_back(v):
    return v

def low_keep(v):
    return (low(v), None)

def low_pass(kept, grad):
    return (grad,)

def back_keep(v):
    return (v, None)

def back_low(kept, grad):
    return (low(grad),)
low.defvjp(low_keep, low_pass)
low_back.defvjp(back_keep, back_low)

def crms(stream_now):
    totals = lax.optimization_barrier(jnp.sum(stream_now, axis=1, keepdims=True))
    squares = lax.optimization_barrier(jnp.sum(stream_now * stream_now, axis=1, keepdims=True))
    return stream_now * lax.rsqrt((squares + totals * totals) / stream_now.shape[1] + EPS)

def group_attention(queries, keys_all, values_all, segment):
    length = queries.shape[0]
    block_rows = min(512, length)
    score_scale = float(queries.shape[2]) ** (-0.5)
    positions = jnp.arange(length, dtype=jnp.int32)

    def one_block(offset):
        query_rows = lax.dynamic_slice_in_dim(queries, offset, block_rows, 0)
        row_segment = lax.dynamic_slice_in_dim(segment, offset, block_rows, 0)
        row_positions = offset + jnp.arange(block_rows, dtype=jnp.int32)
        scores = low_back(jnp.einsum('qhe,khe->hqk', query_rows, keys_all, precision=HIGH) * score_scale)
        allowed = (row_segment[:, None] == segment[None, :]) & (row_positions[:, None] >= positions[None, :])
        scores = jnp.where(allowed[None], scores, -1e+30)
        chances = low(jax.nn.softmax(scores, axis=2))
        return jnp.einsum('hqk,khe->qhe', chances, values_all, precision=HIGH)
    offsets = jnp.arange(length // block_rows, dtype=jnp.int32) * block_rows
    result = lax.map(jax.checkpoint(one_block), offsets)
    return result.reshape(length, queries.shape[1], queries.shape[2])

def attend_group(member):
    return group_attention(member[0], member[1], member[2], member[3])

def layer_forward(stream_now, segment, column_keep, w_qkv, b_qv, w_out, b_out, w_up, b_up, w_down, b_down):
    tokens, full_width = stream_now.shape
    head_size = full_width // HEADS
    groups = segment.shape[0]
    normed = low(crms(stream_now))
    projected = jnp.einsum('td,dce->tce', normed, w_qkv, precision=HIGH)
    queries = low(low_back(projected[:, 0] + b_qv[0]))
    keys_now = low(low_back(projected[:, 1]))
    values_now = low(low_back(projected[:, 2] + b_qv[1]))
    grouped = (groups, tokens // groups, HEADS, head_size)
    attended = lax.map(attend_group, (queries.reshape(grouped), keys_now.reshape(grouped), values_now.reshape(grouped), segment))
    mixed_heads = low(low_back(attended.reshape(tokens, full_width)))
    branch = jnp.dot(mixed_heads, w_out, precision=HIGH, preferred_element_type=jnp.float32) + b_out
    middle = stream_now + low_back(branch * column_keep)
    normed_second = low(crms(middle))
    hidden = low_back(jnp.dot(normed_second, w_up, precision=HIGH, preferred_element_type=jnp.float32) + b_up)
    active = low(jax.nn.gelu(hidden, approximate=True))
    branch_two = jnp.dot(active, w_down, precision=HIGH, preferred_element_type=jnp.float32) + b_down
    return middle + low_back(branch_two * column_keep)

def reference(stream, seq_lens, w_qkv, b_qv, w_out, b_out, w_up, b_up, w_down, b_down, cotangent):
    full_width = stream.shape[1]
    column_keep = (jnp.arange(full_width, dtype=jnp.int32) < full_width - 1).astype(jnp.float32)
    lengths = seq_lens.reshape(-1, SLOTS)
    bounds = jnp.cumsum(lengths, axis=1, dtype=jnp.int32)
    positions = jnp.arange(TOK_DEV, dtype=jnp.int32)
    segment = lax.optimization_barrier(jnp.sum((positions[None, :, None] >= bounds[:, None, :-1]).astype(jnp.int32), axis=2, dtype=jnp.int32))
    weights = tuple((member.astype(jnp.float32) for member in (w_qkv, b_qv, w_out, b_out, w_up, b_up, w_down, b_down)))

    def forward(stream_in, wq_all, bq_all, wo_all, bo_all, wu_all, bu_all, wd_all, bd_all):
        stream_now = stream_in * column_keep
        layer_outs = []
        for layer_index in range(LAYERS):
            stream_now = layer_forward(stream_now, segment, column_keep, wq_all[layer_index], bq_all[layer_index], wo_all[layer_index], bo_all[layer_index], wu_all[layer_index], bu_all[layer_index], wd_all[layer_index], bd_all[layer_index])
            layer_outs.append(stream_now)
        return (layer_outs[-1], layer_outs[0])
    second_out, pullback, first_out = jax.vjp(forward, stream, *weights, has_aux=True)
    gradients = pullback(cotangent)
    return (first_out, second_out, gradients[0], gradients[1], gradients[2], gradients[3], gradients[4], gradients[5], gradients[6], gradients[7], gradients[8])
```

```python
import functools

import jax
import jax.numpy as jnp
from jax import lax
from jax.experimental import pallas as pl
from jax.experimental.pallas import tpu as pltpu
from jax.sharding import Mesh, PartitionSpec as P

HEADS = 12
EPS = 1e-06
ROWS_T = (((0,), (0,)), ((), ()))
COLS_T = (((1,), (1,)), ((), ()))
NEG = -1e30
AXES = ("g", "p", "c", "mp")
PIECES = 4
bf16 = jnp.bfloat16
f32 = jnp.float32


def dot_nt(a, b):
    return lax.dot_general(a, b, COLS_T, preferred_element_type=f32)


def dot_tn(a, b):
    return lax.dot_general(a, b, ROWS_T, preferred_element_type=f32)


def dot_nn(a, b):
    return jnp.dot(a, b, preferred_element_type=f32)


def lane_mask(head, half):
    lanes = lax.broadcasted_iota(jnp.int32, (1, 2 * half), 1)
    return (lanes < half) if head == 0 else (lanes >= half)


def pick(mask, values):
    return jnp.where(mask, values, jnp.zeros_like(values))


def fwd_block(q, k, v, half, diagonal):
    out = None
    highs = []
    sums = []
    for head in (0, 1):
        mask = lane_mask(head, half)
        scores = dot_nt(q, pick(mask, k))
        if diagonal:
            rows = lax.broadcasted_iota(jnp.int32, scores.shape, 0)
            cols = lax.broadcasted_iota(jnp.int32, scores.shape, 1)
            scores = jnp.where(rows >= cols, scores, NEG)
        high = jnp.max(scores, axis=1, keepdims=True)
        chance = jnp.exp(scores - high)
        sums.append(jnp.sum(chance, axis=1, keepdims=True))
        highs.append(high)
        part = dot_nn(chance.astype(bf16), pick(mask, v))
        out = part if out is None else out + part
    first = lane_mask(0, half)
    shape = out.shape
    high = jnp.where(first, jnp.broadcast_to(highs[0], shape), jnp.broadcast_to(highs[1], shape))
    total = jnp.where(first, jnp.broadcast_to(sums[0], shape), jnp.broadcast_to(sums[1], shape))
    return out, high, total


def merge_into(acc_ref, high_ref, sum_ref, rows, part):
    out, high, total = part
    old = high_ref[rows, :]
    new = jnp.maximum(old, high)
    keep = jnp.exp(old - new)
    take = jnp.exp(high - new)
    acc_ref[rows, :] = acc_ref[rows, :] * keep + out * take
    sum_ref[rows, :] = sum_ref[rows, :] * keep + total * take
    high_ref[rows, :] = new


def fwd_local_kernel(quarter, half, s_ref, q_ref, k_ref, v_ref, acc_ref, high_ref, sum_ref):
    for i in (0, 1):
        rows = pl.ds(i * quarter, quarter)
        out, high, total = fwd_block(q_ref[rows, :], k_ref[rows, :], v_ref[rows, :], half, True)
        acc_ref[rows, :] = out
        high_ref[rows, :] = high
        sum_ref[rows, :] = total

    @pl.when(s_ref[0] > 0)
    def _():
        early = pl.ds(0, quarter)
        late = pl.ds(quarter, quarter)
        part = fwd_block(q_ref[late, :], k_ref[early, :], v_ref[early, :], half, False)
        merge_into(acc_ref, high_ref, sum_ref, late, part)


def fwd_remote_kernel(
    quarter, half, s_ref, q_ref, k_ref, v_ref, acc_in, high_in, sum_in, out_ref, lse_ref, acc_ref, high_ref, sum_ref
):
    acc_ref[...] = acc_in[...]
    high_ref[...] = high_in[...]
    sum_ref[...] = sum_in[...]

    @pl.when(s_ref[0] > 0)
    def _():
        early = pl.ds(0, quarter)
        late = pl.ds(quarter, quarter)
        part = fwd_block(q_ref[late, :], k_ref[early, :], v_ref[early, :], half, False)
        merge_into(acc_ref, high_ref, sum_ref, late, part)
        which = pl.ds(pl.multiple_of(s_ref[1] * quarter, quarter), quarter)
        part = fwd_block(q_ref[which, :], k_ref[which, :], v_ref[which, :], half, False)
        merge_into(acc_ref, high_ref, sum_ref, which, part)

    total = sum_ref[...]
    out_ref[...] = (acc_ref[...] / total).astype(out_ref.dtype)
    lse = high_ref[...] + jnp.log(total)
    flat = lse.T
    lse_ref[0, 0:1, :] = flat[0:1, :]
    lse_ref[0, 1:2, :] = flat[half : half + 1, :]


def bwd_block(q, do, k, v, lse, inner, half, diagonal):
    k_t = k.T
    d_key = d_value = d_query_t = None
    subl = lax.broadcasted_iota(jnp.int32, (2 * half, 1), 0)
    for head in (0, 1):
        mask = lane_mask(head, half)
        scores = dot_nt(pick(mask, k), q)
        chance = jnp.exp(scores - lse[head : head + 1, :])
        if diagonal:
            keys = lax.broadcasted_iota(jnp.int32, scores.shape, 0)
            queries = lax.broadcasted_iota(jnp.int32, scores.shape, 1)
            chance = jnp.where(queries >= keys, chance, 0.0)
        d_chance = dot_nt(pick(mask, v), do)
        d_scores = (chance * (d_chance - inner[head : head + 1, :])).astype(bf16)
        part_v = dot_nn(chance.astype(bf16), pick(mask, do))
        part_k = dot_nn(d_scores, pick(mask, q))
        row_mask = (subl < half) if head == 0 else (subl >= half)
        part_q = dot_nn(pick(row_mask, k_t), d_scores)
        d_value = part_v if d_value is None else d_value + part_v
        d_key = part_k if d_key is None else d_key + part_k
        d_query_t = part_q if d_query_t is None else d_query_t + part_q
    return d_query_t, d_key, d_value


def bwd_remote_kernel(
    quarter, half, s_ref, q_ref, k_ref, v_ref, o_ref, do_ref, lse_ref, dqt_ref, dk_ref, dv_ref, inner_ref, ak_ref, av_ref
):
    flat = (o_ref[...].astype(f32) * do_ref[...].astype(f32)).T
    inner_ref[0, 0:1, :] = jnp.sum(flat[:half, :], axis=0, keepdims=True)
    inner_ref[0, 1:2, :] = jnp.sum(flat[half:, :], axis=0, keepdims=True)
    dqt_ref[...] = jnp.zeros_like(dqt_ref)
    ak_ref[...] = jnp.zeros_like(ak_ref)
    av_ref[...] = jnp.zeros_like(av_ref)

    @pl.when(s_ref[0] > 0)
    def _():
        def job(q_rows, k_rows):
            dqt, dk, dv = bwd_block(
                q_ref[q_rows, :],
                do_ref[q_rows, :],
                k_ref[k_rows, :],
                v_ref[k_rows, :],
                lse_ref[0, 0:2, q_rows],
                inner_ref[0, 0:2, q_rows],
                half,
                False,
            )
            dqt_ref[0, :, q_rows] += dqt
            ak_ref[k_rows, :] += dk
            av_ref[k_rows, :] += dv

        job(pl.ds(quarter, quarter), pl.ds(0, quarter))
        which = pl.ds(pl.multiple_of(s_ref[1] * quarter, quarter), quarter)
        job(which, which)

    dk_ref[...] = ak_ref[...].astype(dk_ref.dtype)
    dv_ref[...] = av_ref[...].astype(dv_ref.dtype)


def bwd_local_kernel(
    quarter, half, scale, s_ref, q_ref, k_ref, v_ref, do_ref, lse_ref, inner_ref, dqt_in, dq_ref, dk_ref, dv_ref, dqt_ref, ak_ref, av_ref
):
    for i in (0, 1):
        rows = pl.ds(i * quarter, quarter)
        dqt, dk, dv = bwd_block(
            q_ref[rows, :], do_ref[rows, :], k_ref[rows, :], v_ref[rows, :],
            lse_ref[0, 0:2, rows], inner_ref[0, 0:2, rows], half, True,
        )
        dqt_ref[:, rows] = dqt_in[0, :, rows] + dqt
        ak_ref[rows, :] = dk
        av_ref[rows, :] = dv

    @pl.when(s_ref[0] > 0)
    def _():
        early = pl.ds(0, quarter)
        late = pl.ds(quarter, quarter)
        dqt, dk, dv = bwd_block(
            q_ref[late, :], do_ref[late, :], k_ref[early, :], v_ref[early, :],
            lse_ref[0, 0:2, late], inner_ref[0, 0:2, late], half, False,
        )
        dqt_ref[:, late] += dqt
        ak_ref[early, :] += dk
        av_ref[early, :] += dv

    dq_ref[...] = (dqt_ref[...].T * scale).astype(dq_ref.dtype)
    dk_ref[...] = ak_ref[...].astype(dk_ref.dtype)
    dv_ref[...] = av_ref[...].astype(dv_ref.dtype)


class Attention:
    def __init__(self, tokens, heads, size):
        self.tokens, self.pairs, self.size = tokens, heads // 2, size
        self.quarter = tokens // 2
        self.width = 2 * size

    def rows(self, first):
        return pl.BlockSpec((self.tokens, self.width), lambda j, s: (0, first + j))

    def flat(self):
        return pl.BlockSpec((1, 8, self.tokens), lambda j, s: (j, 0, 0))

    def turned(self):
        return pl.BlockSpec((1, self.width, self.tokens), lambda j, s: (j, 0, 0))

    def call(self, kernel, in_specs, out_specs, out_shape, scratch, blocks, dots):
        flops = blocks * dots * 2 * self.quarter * self.quarter * self.width * 2 * self.pairs
        return pl.pallas_call(
            kernel,
            out_shape=out_shape,
            grid_spec=pltpu.PrefetchScalarGridSpec(
                num_scalar_prefetch=1,
                grid=(self.pairs,),
                in_specs=in_specs,
                out_specs=out_specs,
                scratch_shapes=scratch,
            ),
            compiler_params=pltpu.CompilerParams(vmem_limit_bytes=40 * 2**20),
            cost_estimate=pl.CostEstimate(
                flops=flops * 2, bytes_accessed=8 * 2**20, transcendentals=blocks * 2 * self.pairs * self.quarter**2
            ),
        )

    def shape(self, dtype):
        return jax.ShapeDtypeStruct((self.tokens, self.pairs * self.width), dtype)

    def flat_shape(self):
        return jax.ShapeDtypeStruct((self.pairs, 8, self.tokens), f32)

    def scratch(self):
        return pltpu.VMEM((self.tokens, self.width), f32)

    def forward_local(self, flags, qkv):
        n = self.pairs
        return self.call(
            functools.partial(fwd_local_kernel, self.quarter, self.size),
            [self.rows(0), self.rows(n), self.rows(2 * n)],
            [self.rows(0)] * 3,
            [self.shape(f32)] * 3,
            [],
            3,
            2,
        )(flags, qkv, qkv, qkv)

    def forward_remote(self, flags, qkv, kv, acc, high, total):
        n = self.pairs
        return self.call(
            functools.partial(fwd_remote_kernel, self.quarter, self.size),
            [self.rows(0), self.rows(0), self.rows(n), self.rows(0), self.rows(0), self.rows(0)],
            [self.rows(0), self.flat()],
            [self.shape(bf16), self.flat_shape()],
            [self.scratch()] * 3,
            2,
            2,
        )(flags, qkv, kv, kv, acc, high, total)

    def backward_remote(self, flags, qkv, kv, out, d_out, lse):
        n = self.pairs
        return self.call(
            functools.partial(bwd_remote_kernel, self.quarter, self.size),
            [self.rows(0), self.rows(0), self.rows(n), self.rows(0), self.rows(0), self.flat()],
            [self.turned(), self.rows(0), self.rows(0), self.flat()],
            [
                jax.ShapeDtypeStruct((n, self.width, self.tokens), f32),
                self.shape(bf16),
                self.shape(bf16),
                self.flat_shape(),
            ],
            [self.scratch()] * 2,
            2,
            5,
        )(flags, qkv, kv, kv, out, d_out, lse)

    def backward_local(self, flags, qkv, d_out, lse, inner, dqt):
        n = self.pairs
        return self.call(
            functools.partial(bwd_local_kernel, self.quarter, self.size, float(self.size) ** -0.5),
            [self.rows(0), self.rows(n), self.rows(2 * n), self.rows(0), self.flat(), self.flat(), self.turned()],
            [self.rows(0)] * 3,
            [self.shape(bf16)] * 3,
            [pltpu.VMEM((self.width, self.tokens), f32), self.scratch(), self.scratch()],
            3,
            5,
        )(flags, qkv, qkv, qkv, d_out, lse, inner, dqt)


class Moves:
    def __init__(self, groups, pieces, chips):
        self.sizes = (groups, pieces, 2, chips)
        self.c = lax.axis_index("c")
        self.z = lax.axis_index("mp")
        self.spot = 2 * (self.z % 2) + self.c

    def permute(self, value, target):
        groups, pieces, cores, chips = self.sizes
        place = lambda g, p, c, z: ((g * pieces + p) * cores + c) * chips + z
        pairs = [
            (place(g, p, c, z), place(*target(g, p, c, z)))
            for g in range(groups)
            for p in range(pieces)
            for c in range(cores)
            for z in range(chips)
        ]
        return lax.ppermute(value, AXES, pairs)

    def core(self, value):
        return self.permute(value, lambda g, p, c, z: (g, p, 1 - c, z))

    def chip(self, value, bit):
        return self.permute(value, lambda g, p, c, z: (g, p, c, z ^ bit))

    def column(self, value, bit):
        return self.permute(value, lambda g, p, c, z: (g, p ^ bit, c, z))

    def both_cores(self, mine, axis=0):
        other = self.core(mine)
        return self.in_order(mine, other, axis)

    def in_order(self, mine, other, axis=0):
        return jnp.where(
            self.c == 0,
            jnp.concatenate([mine, other], axis=axis),
            jnp.concatenate([other, mine], axis=axis),
        )

    @staticmethod
    def shuffle(blocks, index):
        odd = (index % 2) == 1
        high = index >= 2
        blocks = [jnp.where(odd, blocks[j ^ 1], blocks[j]) for j in range(4)]
        return [jnp.where(high, blocks[j ^ 2], blocks[j]) for j in range(4)]

    def to_rows(self, block):
        quarter = block.shape[0] // 4
        got = []
        for k in range(4):
            spot = self.z ^ k
            which = jnp.where(spot == 0, 0, jnp.where(spot == 1, 3, spot - 1))
            send = lax.dynamic_slice_in_dim(block, which * quarter, quarter, 0).astype(bf16)

            def target(g, p, c, z, k=k):
                t = z ^ k
                return (g, p, t % 2, 2 * c + t // 2)

            got.append(self.permute(send, target))
        return jnp.concatenate(self.shuffle(got, self.spot), axis=1)

    def to_columns(self, rows):
        width = rows.shape[1] // 4
        blocks = [rows[:, j * width : (j + 1) * width].astype(bf16) for j in range(4)]
        blocks = self.shuffle(blocks, self.spot)
        got = []
        for k in range(4):

            def target(g, p, c, z, k=k):
                t = 2 * (z % 2) + c
                return (g, p, z // 2, t ^ k)

            got.append(self.permute(blocks[k], target))
        parts = self.shuffle(got, self.z)
        return jnp.concatenate([parts[0], parts[2], parts[3], parts[1]], axis=0).astype(f32)


def norm(stream):
    total = jnp.sum(stream, axis=1, keepdims=True)
    squares = jnp.sum(stream * stream, axis=1, keepdims=True)
    factor = lax.rsqrt((squares + total * total) / stream.shape[1] + EPS)
    return total, factor, (stream * factor).astype(bf16)


def norm_back(stream, total, factor, d_normed):
    inner = jnp.sum(d_normed * stream, axis=1, keepdims=True)
    term = factor * factor * factor * inner / stream.shape[1]
    return factor * d_normed - term * (stream + total)


def gelu_parts(x):
    a = 0.7978845608028654
    t = jnp.tanh(a * (x + 0.044715 * (x * x * x)))
    value = 0.5 * x * (1.0 + t)
    slope = 0.5 * (1.0 + t) + 0.5 * x * (1.0 - t * t) * (a * (1.0 + 3 * 0.044715 * (x * x)))
    return value.astype(bf16), slope.astype(bf16)


def per_device(stream, seq_lens, w_qkv, b_qv, w_out, b_out, w_up, b_up, w_down, b_down, cotangent):
    groups = lax.axis_size("g")
    mv = Moves(groups, lax.axis_size("p"), lax.axis_size("mp"))
    c, z = mv.c, mv.z
    piece = lax.axis_index("p") * 2 + c
    length, local = stream.shape
    chips = lax.axis_size("mp")
    width = local * chips
    layers = w_qkv.shape[0]
    hidden = w_up.shape[2]
    size = width // HEADS
    quarter = length // 4
    tokens = 2 * quarter
    att = Attention(tokens, HEADS // 2, size)
    keep = (jnp.arange(width, dtype=jnp.int32) < width - 1).astype(f32)[None, :]
    keep16 = keep.astype(bf16)
    step = hidden // (2 * PIECES)
    part = local // (2 * PIECES)

    lens_other = mv.core(seq_lens)
    lens = jnp.where(c == z // 2, seq_lens, lens_other)
    flags = jnp.stack([(lens[0] > quarter).astype(jnp.int32), 1 - z % 2])

    flat = jnp.concatenate([b_qv.reshape(-1), b_out.reshape(-1), b_up.reshape(-1), b_down.reshape(-1)])[None]
    other = mv.chip(flat, 1)
    pair = jnp.where(z % 2 == 0, jnp.concatenate([flat, other]), jnp.concatenate([other, flat]))
    other = mv.chip(pair, 2)
    biases = jnp.where(z < 2, jnp.concatenate([pair, other]), jnp.concatenate([other, pair]))
    cuts = [0, layers * 2 * local, layers * local, layers * hidden, layers * local]
    ends = [sum(cuts[: i + 1]) for i in range(5)]

    def bias(i, shape):
        return biases[:, ends[i] : ends[i + 1]].reshape((chips,) + shape)

    all_qv = bias(0, (layers, 2, local))
    all_qv = lax.dynamic_slice_in_dim(all_qv, 2 * c, 2, 0)
    bias_qv = jnp.transpose(all_qv, (1, 2, 0, 3)).reshape(layers, 2, 2 * local)
    bias_out = jnp.transpose(bias(1, (layers, local)), (1, 0, 2)).reshape(layers, width)
    bias_down = jnp.transpose(bias(3, (layers, local)), (1, 0, 2)).reshape(layers, width)
    all_up = bias(2, (layers, PIECES, 2, step))
    all_up = lax.dynamic_index_in_dim(all_up, c, 3, keepdims=False)
    bias_up = jnp.transpose(all_up, (1, 2, 0, 3)).reshape(layers, chips * PIECES * step)

    def gather_heads(kinds):
        count = kinds.shape[0]
        cut = kinds.reshape(count, PIECES, 2, part, width)
        mine = lax.dynamic_index_in_dim(cut, c, 2, keepdims=False).reshape(count * PIECES * part, width)
        every = lax.all_gather(mine, "mp", axis=0, tiled=True).reshape(2, 2, count, PIECES, part, width)
        got = mv.core(lax.dynamic_index_in_dim(every, 1 - c, 0, keepdims=False))
        own = lax.dynamic_index_in_dim(every, c, 0, keepdims=False)
        whole = mv.in_order(own[:, :, :, None], got[:, :, :, None], axis=3)
        return jnp.transpose(whole, (1, 0, 2, 3, 4, 5)).reshape(count, 2 * local, width)

    def gather_units(rows):
        return lax.all_gather(lax.all_gather(rows, "mp", axis=0, tiled=True), "p", axis=0, tiled=True)

    def turned_qkv(layer):
        return jnp.transpose(w_qkv[layer], (1, 2, 0))

    qkv_rows, out_rows, up_rows, down_rows = [], [], [], []
    for layer in range(layers):
        if layer == 0:
            qkv_rows.append(gather_heads(turned_qkv(layer)).reshape(6 * local, width))
            out_rows.append(gather_heads(w_out[layer][None])[0])
        else:
            both = gather_heads(jnp.concatenate([turned_qkv(layer), w_out[layer][None]]))
            qkv_rows.append(both[:3].reshape(6 * local, width))
            out_rows.append(both[3])
        up_rows.append(gather_units(lax.dynamic_slice_in_dim(w_up[layer], piece * step, step, 1).T))
        down_rows.append(gather_units(lax.dynamic_slice_in_dim(w_down[layer], piece * step, step, 0)))

    x = mv.both_cores(mv.to_rows(stream)).astype(f32) * keep
    saved = []
    outs = []
    half_heads = 2 * local
    for layer in range(layers):
        total, factor, n = norm(x)
        n_mine = lax.dynamic_slice_in_dim(n, c * quarter, quarter, 0)
        n_far = mv.both_cores(mv.chip(n_mine, 1))
        scale = float(size) ** -0.5
        proj = dot_nt(n, qkv_rows[layer])
        zero = jnp.zeros((half_heads,), f32)
        add = jnp.concatenate([bias_qv[layer, 0], zero, bias_qv[layer, 1]])
        mult = jnp.concatenate([zero + scale, zero + 1.0, zero + 1.0])
        qkv = ((proj + add).astype(bf16).astype(f32) * mult).astype(bf16)
        acc, high, sums = att.forward_local(flags, qkv)
        kv = (dot_nt(n_far, qkv_rows[layer][half_heads:]) + add[half_heads:]).astype(bf16)
        o, lse = att.forward_remote(flags, qkv, kv, acc, high, sums)
        branch = dot_nn(o, out_rows[layer]).astype(bf16)
        branch = branch.astype(f32) + mv.core(branch).astype(f32)
        x1 = x + (branch + bias_out[layer]) * keep
        total1, factor1, n1 = norm(x1)
        g, slope = gelu_parts(dot_nt(n1, up_rows[layer]) + bias_up[layer])
        branch = dot_nn(g, down_rows[layer]).astype(bf16)
        branch = branch.astype(f32) + mv.core(branch).astype(f32)
        saved.append((x, total, factor, n, n_far, qkv, kv, o, lse, x1, total1, factor1, n1, g, slope))
        x = x1 + (branch + bias_down[layer]) * keep
        outs.append(lax.dynamic_slice_in_dim(x, c * quarter, quarter, 0))

    def finish_sum(value):
        value = lax.psum_scatter(value, "mp", scatter_dimension=0, tiled=True)
        if groups > 1:
            value = lax.psum(value, "g")
        return lax.all_gather(value, ("p", "c"), axis=0, tiled=True)

    def sum_units(rows):
        return finish_sum(lax.psum_scatter(rows.astype(bf16), "p", scatter_dimension=0, tiled=True)).astype(f32)

    def sum_heads(kinds):
        count = kinds.shape[0]
        cut = kinds.astype(bf16).reshape(count, 2, PIECES, 2, part, width)
        mine = lax.dynamic_index_in_dim(cut, c, 3, keepdims=False)
        got = mv.core(lax.dynamic_index_in_dim(cut, 1 - c, 3, keepdims=False))
        whole = mv.in_order(mine, got, axis=1)
        whole = jnp.transpose(whole, (2, 1, 0, 3, 4)).reshape(-1, width)
        done = finish_sum(lax.psum_scatter(whole, "p", scatter_dimension=0, tiled=True))
        done = jnp.transpose(done.reshape(PIECES, 2, count, part, width), (2, 0, 1, 3, 4))
        return done.reshape(count, local, width).astype(f32)

    dx = mv.both_cores(mv.to_rows(cotangent)).astype(f32)
    late = None
    gw_qkv, gw_out, gw_up, gw_down = {}, {}, {}, {}
    gb_qv, gb_out, gb_up, gb_down = {}, {}, {}, {}
    for layer in reversed(range(layers)):
        x, total, factor, n, n_far, qkv, kv, o, lse, x1, total1, factor1, n1, g, slope = saved[layer]
        dm = dx.astype(bf16) * keep16
        gb_down[layer] = jnp.sum(dm, axis=0, dtype=f32)
        gw_down[layer] = sum_units(dot_tn(g, dm))
        dh = (dot_nt(dm, down_rows[layer]) * slope.astype(f32)).astype(bf16)
        gb_up[layer] = jnp.sum(dh, axis=0, dtype=f32)
        gw_up[layer] = sum_units(dot_tn(dh, n1)).T
        dn1 = dot_nn(dh, up_rows[layer]).astype(bf16)
        dn1 = dn1.astype(f32) + mv.core(dn1).astype(f32)
        dx1 = dx + norm_back(x1, total1, factor1, dn1)
        da = dx1.astype(bf16) * keep16
        gb_out[layer] = jnp.sum(da, axis=0, dtype=f32)
        g_out = dot_tn(o, da)
        do = dot_nt(da, out_rows[layer]).astype(bf16)
        dqt, dkr, dvr, inner = att.backward_remote(flags, qkv, kv, o, do, lse)
        dkv = jnp.concatenate([dkr, dvr], axis=1)
        far = dot_nn(dkv, qkv_rows[layer][half_heads:]).astype(bf16)
        far_got = mv.core(lax.dynamic_slice_in_dim(far, (1 - c) * quarter, quarter, 0))
        far_mine = lax.dynamic_slice_in_dim(far, c * quarter, quarter, 0)
        far_sum = (far_mine.astype(f32) + far_got.astype(f32)).astype(bf16)
        back = mv.chip(far_sum, 1)
        dq, dk, dv = att.backward_local(flags, qkv, do, lse, inner, dqt)
        dqkv = jnp.concatenate([dq, dk, dv], axis=1)
        gb_qv[layer] = jnp.stack(
            [
                jnp.sum(dq, axis=0, dtype=f32),
                jnp.sum(dv, axis=0, dtype=f32) + jnp.sum(dvr, axis=0, dtype=f32),
            ]
        )
        g_qkv = jnp.concatenate(
            [dot_tn(dq, n), dot_tn(dkv, n_far) + dot_tn(dqkv[:, half_heads:], n)]
        ).reshape(3, half_heads, width)
        if layer > 0:
            late = jnp.concatenate([g_qkv, g_out[None]])
            if layer > 1:
                late = None
                done = sum_heads(jnp.concatenate([g_qkv, g_out[None]]))
                gw_qkv[layer], gw_out[layer] = done[:3], done[3]
            else:
                held = late
        else:
            if layers > 1:
                done = sum_heads(jnp.concatenate([held, g_out[None]]))
                gw_qkv[1], gw_out[1], gw_out[0] = done[:3], done[3], done[4]
                gw_qkv[0] = sum_heads(g_qkv)
            else:
                done = sum_heads(jnp.concatenate([g_qkv, g_out[None]]))
                gw_qkv[0], gw_out[0] = done[:3], done[3]
        dn = dot_nn(dqkv, qkv_rows[layer])
        zero_rows = jnp.zeros_like(back)
        wide = jnp.where(
            c == 0, jnp.concatenate([back, zero_rows]), jnp.concatenate([zero_rows, back])
        )
        dn = (dn + wide.astype(f32)).astype(bf16)
        dn = dn.astype(f32) + mv.core(dn).astype(f32)
        dx = dx1 + norm_back(x, total, factor, dn)

    grad_stream = mv.to_columns(lax.dynamic_slice_in_dim(dx * keep, c * quarter, quarter, 0))
    outs = [mv.to_columns(value) for value in outs]

    once = (c == 0).astype(f32)

    def by_chip(value):
        return jnp.transpose(value.reshape(layers, chips, local) * once, (1, 0, 2)).reshape(chips, -1)

    qv = jnp.stack([gb_qv[i] for i in range(layers)]).reshape(layers, 2, 2, local)
    qv = jnp.transpose(qv, (2, 0, 1, 3)).reshape(2, -1)
    none = jnp.zeros_like(qv)
    qv = jnp.where(c == 0, jnp.concatenate([qv, none]), jnp.concatenate([none, qv]))
    up = jnp.stack([gb_up[i] for i in range(layers)]).reshape(layers, PIECES, chips, step)
    up = jnp.transpose(up, (2, 0, 1, 3))[:, :, :, None]
    none = jnp.zeros_like(up)
    up = jnp.where(c == 0, jnp.concatenate([up, none], axis=3), jnp.concatenate([none, up], axis=3))
    flat = jnp.concatenate(
        [
            qv,
            by_chip(jnp.stack([gb_out[i] for i in range(layers)])),
            up.reshape(chips, -1),
            by_chip(jnp.stack([gb_down[i] for i in range(layers)])),
        ],
        axis=1,
    )
    flat = flat + mv.core(flat)
    flat = flat + mv.column(flat, 1)
    flat = flat + mv.column(flat, 2)
    flat = flat + mv.chip(flat, 1)
    flat = flat + mv.chip(flat, 2)
    if groups > 1:
        flat = lax.psum(flat, "g")
    flat = lax.dynamic_index_in_dim(flat, z, 0, keepdims=False)
    pieces = [flat[ends[i] : ends[i + 1]] for i in range(4)]
    every = range(layers)
    return (
        outs[0],
        outs[-1],
        grad_stream,
        jnp.stack([jnp.transpose(gw_qkv[i], (2, 0, 1)) for i in every]),
        pieces[0].reshape(layers, 2, local),
        jnp.stack([gw_out[i] for i in every]),
        pieces[1].reshape(layers, local),
        jnp.stack([gw_up[i] for i in every]),
        pieces[2].reshape(layers, hidden),
        jnp.stack([gw_down[i] for i in every]),
        pieces[3].reshape(layers, local),
    )


def solution(mesh):
    rows, chips = mesh.shape["dp"], mesh.shape["mp"]
    grid = Mesh(mesh.devices.reshape(rows // (2 * PIECES), PIECES, 2, chips), AXES)
    dp = ("g", "p", "c")
    in_specs = (
        P(dp, "mp"),
        P(dp),
        P(None, None, None, "mp"),
        P(None, None, "mp"),
        P(None, "mp", None),
        P(None, "mp"),
        P(None, None, "mp"),
        P(None, "mp"),
        P(None, "mp", None),
        P(None, "mp"),
        P(dp, "mp"),
    )
    out_specs = (
        P(dp, "mp"),
        P(dp, "mp"),
        P(dp, "mp"),
        P(None, None, None, "mp"),
        P(None, None, "mp"),
        P(None, "mp", None),
        P(None, "mp"),
        P(None, None, "mp"),
        P(None, "mp"),
        P(None, "mp", None),
        P(None, "mp"),
    )
    return jax.shard_map(per_device, mesh=grid, in_specs=in_specs, out_specs=out_specs, check_vma=False)
```

```python
import functools

import jax
import jax.numpy as jnp
from jax import lax
from jax.experimental import pallas as pl
from jax.experimental.pallas import tpu as pltpu
from jax.sharding import Mesh, PartitionSpec as P

HEADS = 12
EPS = 1e-06
ROWS_T = (((0,), (0,)), ((), ()))
COLS_T = (((1,), (1,)), ((), ()))
NEG = -1e30
AXES = ("g", "p", "c", "mp")
PIECES = 4
COST = 1.0
VMEM = 58 * 2**20
bf16 = jnp.bfloat16
f32 = jnp.float32


def dot_nt(a, b):
    return lax.dot_general(a, b, COLS_T, preferred_element_type=f32)


def dot_tn(a, b):
    return lax.dot_general(a, b, ROWS_T, preferred_element_type=f32)


def dot_nn(a, b):
    return jnp.dot(a, b, preferred_element_type=f32)


def cost(us):
    return pl.CostEstimate(flops=int(us * 1e9 * COST), bytes_accessed=int(us * 3e6 * COST), transcendentals=0)


def lane_mask(head, half):
    lanes = lax.broadcasted_iota(jnp.int32, (1, 2 * half), 1)
    return (lanes < half) if head == 0 else (lanes >= half)


def pick(mask, values):
    return jnp.where(mask, values, jnp.zeros_like(values))


def fwd_block(q, k, v, half, diagonal):
    out = None
    highs = []
    sums = []
    for head in (0, 1):
        mask = lane_mask(head, half)
        scores = dot_nt(q, pick(mask, k))
        if diagonal:
            rows = lax.broadcasted_iota(jnp.int32, scores.shape, 0)
            cols = lax.broadcasted_iota(jnp.int32, scores.shape, 1)
            scores = jnp.where(rows >= cols, scores, NEG)
        high = jnp.max(scores, axis=1, keepdims=True)
        chance = jnp.exp(scores - high)
        sums.append(jnp.sum(chance, axis=1, keepdims=True))
        highs.append(high)
        part = dot_nn(chance.astype(bf16), pick(mask, v))
        out = part if out is None else out + part
    first = lane_mask(0, half)
    shape = out.shape
    high = jnp.where(first, jnp.broadcast_to(highs[0], shape), jnp.broadcast_to(highs[1], shape))
    total = jnp.where(first, jnp.broadcast_to(sums[0], shape), jnp.broadcast_to(sums[1], shape))
    return out, high, total


def merge_into(acc_ref, high_ref, sum_ref, rows, part):
    out, high, total = part
    old = high_ref[rows, :]
    new = jnp.maximum(old, high)
    keep = jnp.exp(old - new)
    take = jnp.exp(high - new)
    acc_ref[rows, :] = acc_ref[rows, :] * keep + out * take
    sum_ref[rows, :] = sum_ref[rows, :] * keep + total * take
    high_ref[rows, :] = new


def fwd_local_kernel(quarter, half, s_ref, q_ref, k_ref, v_ref, acc_ref, high_ref, sum_ref):
    for i in (0, 1):
        rows = pl.ds(i * quarter, quarter)
        out, high, total = fwd_block(q_ref[rows, :], k_ref[rows, :], v_ref[rows, :], half, True)
        acc_ref[rows, :] = out
        high_ref[rows, :] = high
        sum_ref[rows, :] = total

    @pl.when(s_ref[0] > 0)
    def _():
        early = pl.ds(0, quarter)
        late = pl.ds(quarter, quarter)
        part = fwd_block(q_ref[late, :], k_ref[early, :], v_ref[early, :], half, False)
        merge_into(acc_ref, high_ref, sum_ref, late, part)


def fwd_remote_kernel(
    quarter, half, s_ref, q_ref, k_ref, v_ref, acc_in, high_in, sum_in, out_ref, lse_ref, acc_ref, high_ref, sum_ref
):
    acc_ref[...] = acc_in[...]
    high_ref[...] = high_in[...]
    sum_ref[...] = sum_in[...]

    @pl.when(s_ref[0] > 0)
    def _():
        early = pl.ds(0, quarter)
        late = pl.ds(quarter, quarter)
        part = fwd_block(q_ref[late, :], k_ref[early, :], v_ref[early, :], half, False)
        merge_into(acc_ref, high_ref, sum_ref, late, part)
        which = pl.ds(pl.multiple_of(s_ref[1] * quarter, quarter), quarter)
        part = fwd_block(q_ref[which, :], k_ref[which, :], v_ref[which, :], half, False)
        merge_into(acc_ref, high_ref, sum_ref, which, part)

    total = sum_ref[...]
    out_ref[...] = (acc_ref[...] / total).astype(out_ref.dtype)
    lse = high_ref[...] + jnp.log(total)
    flat = lse.T
    lse_ref[0, 0:1, :] = flat[0:1, :]
    lse_ref[0, 1:2, :] = flat[half : half + 1, :]


def bwd_block(q, do, k, v, lse, inner, half, diagonal):
    k_t = k.T
    d_key = d_value = d_query_t = None
    subl = lax.broadcasted_iota(jnp.int32, (2 * half, 1), 0)
    for head in (0, 1):
        mask = lane_mask(head, half)
        scores = dot_nt(pick(mask, k), q)
        chance = jnp.exp(scores - lse[head : head + 1, :])
        if diagonal:
            keys = lax.broadcasted_iota(jnp.int32, scores.shape, 0)
            queries = lax.broadcasted_iota(jnp.int32, scores.shape, 1)
            chance = jnp.where(queries >= keys, chance, 0.0)
        d_chance = dot_nt(pick(mask, v), do)
        d_scores = (chance * (d_chance - inner[head : head + 1, :])).astype(bf16)
        part_v = dot_nn(chance.astype(bf16), pick(mask, do))
        part_k = dot_nn(d_scores, pick(mask, q))
        row_mask = (subl < half) if head == 0 else (subl >= half)
        part_q = dot_nn(pick(row_mask, k_t), d_scores)
        d_value = part_v if d_value is None else d_value + part_v
        d_key = part_k if d_key is None else d_key + part_k
        d_query_t = part_q if d_query_t is None else d_query_t + part_q
    return d_query_t, d_key, d_value


def bwd_remote_kernel(
    quarter, half, s_ref, q_ref, k_ref, v_ref, o_ref, do_ref, lse_ref,
    dqt_ref, dk_ref, dv_ref, inner_ref, sums_ref, ak_ref, av_ref
):
    flat = (o_ref[...].astype(f32) * do_ref[...].astype(f32)).T
    inner_ref[0, 0:1, :] = jnp.sum(flat[:half, :], axis=0, keepdims=True)
    inner_ref[0, 1:2, :] = jnp.sum(flat[half:, :], axis=0, keepdims=True)
    dqt_ref[...] = jnp.zeros_like(dqt_ref)
    ak_ref[...] = jnp.zeros_like(ak_ref)
    av_ref[...] = jnp.zeros_like(av_ref)

    @pl.when(s_ref[0] > 0)
    def _():
        def job(q_rows, k_rows):
            dqt, dk, dv = bwd_block(
                q_ref[q_rows, :],
                do_ref[q_rows, :],
                k_ref[k_rows, :],
                v_ref[k_rows, :],
                lse_ref[0, 0:2, q_rows],
                inner_ref[0, 0:2, q_rows],
                half,
                False,
            )
            dqt_ref[0, :, q_rows] += dqt
            ak_ref[k_rows, :] += dk
            av_ref[k_rows, :] += dv

        job(pl.ds(quarter, quarter), pl.ds(0, quarter))
        which = pl.ds(pl.multiple_of(s_ref[1] * quarter, quarter), quarter)
        job(which, which)

    dk_ref[...] = ak_ref[...].astype(dk_ref.dtype)
    dv_ref[...] = av_ref[...].astype(dv_ref.dtype)
    sums_ref[0, 0:1, :] = jnp.sum(av_ref[...], axis=0, keepdims=True)


def bwd_local_kernel(
    quarter, half, scale, s_ref, q_ref, k_ref, v_ref, do_ref, lse_ref, inner_ref, dqt_in,
    dq_ref, dk_ref, dv_ref, sums_ref, dqt_ref, ak_ref, av_ref
):
    for i in (0, 1):
        rows = pl.ds(i * quarter, quarter)
        dqt, dk, dv = bwd_block(
            q_ref[rows, :], do_ref[rows, :], k_ref[rows, :], v_ref[rows, :],
            lse_ref[0, 0:2, rows], inner_ref[0, 0:2, rows], half, True,
        )
        dqt_ref[:, rows] = dqt_in[0, :, rows] + dqt
        ak_ref[rows, :] = dk
        av_ref[rows, :] = dv

    @pl.when(s_ref[0] > 0)
    def _():
        early = pl.ds(0, quarter)
        late = pl.ds(quarter, quarter)
        dqt, dk, dv = bwd_block(
            q_ref[late, :], do_ref[late, :], k_ref[early, :], v_ref[early, :],
            lse_ref[0, 0:2, late], inner_ref[0, 0:2, late], half, False,
        )
        dqt_ref[:, late] += dqt
        ak_ref[early, :] += dk
        av_ref[early, :] += dv

    dq = dqt_ref[...].T * scale
    dq_ref[...] = dq.astype(dq_ref.dtype)
    dk_ref[...] = ak_ref[...].astype(dk_ref.dtype)
    dv_ref[...] = av_ref[...].astype(dv_ref.dtype)
    sums_ref[0, 0:1, :] = jnp.sum(dq, axis=0, keepdims=True)
    sums_ref[0, 1:2, :] = jnp.sum(av_ref[...], axis=0, keepdims=True)


class Attention:
    def __init__(self, tokens, heads, size):
        self.tokens, self.pairs, self.size = tokens, heads // 2, size
        self.quarter = tokens // 2
        self.width = 2 * size

    def rows(self, first):
        return pl.BlockSpec((self.tokens, self.width), lambda j, s: (0, first + j))

    def flat(self):
        return pl.BlockSpec((1, 8, self.tokens), lambda j, s: (j, 0, 0))

    def small(self):
        return pl.BlockSpec((1, 8, self.width), lambda j, s: (j, 0, 0))

    def turned(self):
        return pl.BlockSpec((1, self.width, self.tokens), lambda j, s: (j, 0, 0))

    def call(self, kernel, in_specs, out_specs, out_shape, scratch, blocks, dots):
        return pl.pallas_call(
            kernel,
            out_shape=out_shape,
            grid_spec=pltpu.PrefetchScalarGridSpec(
                num_scalar_prefetch=1,
                grid=(self.pairs,),
                in_specs=in_specs,
                out_specs=out_specs,
                scratch_shapes=scratch,
            ),
            compiler_params=pltpu.CompilerParams(vmem_limit_bytes=VMEM),
            cost_estimate=cost(blocks * dots * 1.2 + 2),
        )

    def shape(self, dtype):
        return jax.ShapeDtypeStruct((self.tokens, self.pairs * self.width), dtype)

    def flat_shape(self):
        return jax.ShapeDtypeStruct((self.pairs, 8, self.tokens), f32)

    def scratch(self):
        return pltpu.VMEM((self.tokens, self.width), f32)

    def forward_local(self, flags, qkv):
        n = self.pairs
        return self.call(
            functools.partial(fwd_local_kernel, self.quarter, self.size),
            [self.rows(0), self.rows(n), self.rows(2 * n)],
            [self.rows(0)] * 3,
            [self.shape(f32)] * 3,
            [],
            3,
            2,
        )(flags, qkv, qkv, qkv)

    def forward_remote(self, flags, qkv, kv, acc, high, total):
        n = self.pairs
        return self.call(
            functools.partial(fwd_remote_kernel, self.quarter, self.size),
            [self.rows(0), self.rows(0), self.rows(n), self.rows(0), self.rows(0), self.rows(0)],
            [self.rows(0), self.flat()],
            [self.shape(bf16), self.flat_shape()],
            [self.scratch()] * 3,
            2,
            2,
        )(flags, qkv, kv, kv, acc, high, total)

    def backward_remote(self, flags, qkv, kv, out, d_out, lse):
        n = self.pairs
        return self.call(
            functools.partial(bwd_remote_kernel, self.quarter, self.size),
            [self.rows(0), self.rows(0), self.rows(n), self.rows(0), self.rows(0), self.flat()],
            [self.turned(), self.rows(0), self.rows(0), self.flat(), self.small()],
            [
                jax.ShapeDtypeStruct((n, self.width, self.tokens), f32),
                self.shape(bf16),
                self.shape(bf16),
                self.flat_shape(),
                jax.ShapeDtypeStruct((n, 8, self.width), f32),
            ],
            [self.scratch()] * 2,
            2,
            5,
        )(flags, qkv, kv, kv, out, d_out, lse)

    def backward_local(self, flags, qkv, d_out, lse, inner, dqt):
        n = self.pairs
        return self.call(
            functools.partial(bwd_local_kernel, self.quarter, self.size, float(self.size) ** -0.5),
            [self.rows(0), self.rows(n), self.rows(2 * n), self.rows(0), self.flat(), self.flat(), self.turned()],
            [self.rows(0)] * 3 + [self.small()],
            [self.shape(bf16)] * 3 + [jax.ShapeDtypeStruct((n, 8, self.width), f32)],
            [pltpu.VMEM((self.width, self.tokens), f32), self.scratch(), self.scratch()],
            3,
            5,
        )(flags, qkv, qkv, qkv, d_out, lse, inner, dqt)


def norm_of(x):
    total = jnp.sum(x, axis=1, keepdims=True)
    squares = jnp.sum(x * x, axis=1, keepdims=True)
    return total, lax.rsqrt((squares + total * total) / x.shape[1] + EPS)


def norm_back(x, d_normed):
    total, factor = norm_of(x)
    inner = jnp.sum(d_normed * x, axis=1, keepdims=True)
    term = factor * factor * factor * inner / x.shape[1]
    return factor * d_normed - term * (x + total)


def chunks(rows, step=128):
    return [pl.ds(i, step) for i in range(0, rows, step)]


def keep_of(width):
    return jnp.where(lax.broadcasted_iota(jnp.int32, (1, width), 1) < width - 1, 1.0, 0.0)


def vmem(count=1):
    return [pl.BlockSpec(memory_space=pltpu.VMEM)] * count


def smem():
    return [pl.BlockSpec(memory_space=pltpu.SMEM)]


def hbm(count=1):
    return [pl.BlockSpec(memory_space=pltpu.HBM)] * count


def shaped(shape, dtype):
    return jax.ShapeDtypeStruct(shape, dtype)


def kernel_call(kernel, us, mib, in_specs, out_specs, out_shape, scratch=(), aliases=None):
    return pl.pallas_call(
        kernel,
        input_output_aliases=aliases or {},
        in_specs=in_specs,
        out_specs=out_specs,
        out_shape=out_shape,
        scratch_shapes=list(scratch),
        compiler_params=pltpu.CompilerParams(vmem_limit_bytes=VMEM),
        cost_estimate=cost(us),
    )


def run(copies, what):
    for copy in copies:
        getattr(copy, what)()


def quarter_kernel(normed, s_ref, *refs):
    blocks, x_ref = refs[:4], refs[4]
    quarter, width = x_ref.shape
    for spot in range(4):

        @pl.when(s_ref[0] == spot)
        def _(spot=spot):
            for rows in chunks(quarter):
                whole = jnp.concatenate([blocks[j ^ spot][rows, :].astype(f32) for j in range(4)], axis=1)
                if normed:
                    whole = whole * keep_of(width)
                    _, factor = norm_of(whole)
                    refs[5][rows, :] = (whole * factor).astype(bf16)
                x_ref[rows, :] = whole.astype(bf16)


def quarter_rows(blocks, spot, normed):
    quarter, part = blocks[0].shape
    shapes = [shaped((quarter, 4 * part), bf16)] * (2 if normed else 1)
    return kernel_call(
        functools.partial(quarter_kernel, normed), 2, 16, smem() + vmem(4), vmem(len(shapes)), shapes
    )(spot[None], *blocks)


def both_kernel(s_ref, mine_ref, other_ref, x_ref, n_ref):
    quarter = mine_ref.shape[0]
    for ref, core in ((mine_ref, s_ref[0]), (other_ref, 1 - s_ref[0])):
        for start in range(0, quarter, 128):
            x = ref[pl.ds(start, 128), :].astype(f32)
            rows = pl.ds(pl.multiple_of(core * quarter + start, 128), 128)
            x_ref[rows, :] = x
            _, factor = norm_of(x)
            n_ref[rows, :] = (x * factor).astype(bf16)


def both_rows(mine, other, core):
    shape = (2 * mine.shape[0], mine.shape[1])
    return kernel_call(both_kernel, 2, 16, smem() + vmem(2), vmem(2), [shaped(shape, f32), shaped(shape, bf16)])(
        core[None], mine, other
    )


class Stage:
    def __init__(self, ins, in_sems, outs, out_sems):
        self.ins = [self.parts(a, b, sem) for (a, b), sem in zip(ins, in_sems)]
        self.outs = [(b, a, sem) for (a, b), sem in zip(outs, out_sems)]
        self.targets = [a for a, _ in outs]
        self.waited = set()
        self.pushed = []
        for copies in self.ins:
            run(copies, "start")

    @staticmethod
    def parts(source, target, sem):
        count = sem.shape[0]
        rows = source.shape[0] // count
        if count == 1:
            return [pltpu.make_async_copy(source, target, sem.at[0])]
        cut = [pl.ds(i * rows, rows) for i in range(count)]
        return [pltpu.make_async_copy(source.at[r], target.at[r], sem.at[i]) for i, r in enumerate(cut)]

    def need(self, *which, part=None):
        for i in which:
            for k, copy in enumerate(self.ins[i]):
                if (part is None or k == part % len(self.ins[i])) and (i, k) not in self.waited:
                    self.waited.add((i, k))
                    copy.wait()

    def push(self, *which, part=0):
        for i in which:
            source, target, sem = self.outs[i]
            rows = source.shape[0] // sem.shape[0]
            cut = pl.ds(part * rows, rows)
            copy = pltpu.make_async_copy(source.at[cut], target.at[cut], sem.at[part])
            copy.start()
            self.pushed.append(copy)

    def done(self):
        run(self.pushed, "wait")


def staged(body, us, scalars, ins, raw, outs, raw_outs=(), small=(), scratch=(), single=False, aliases=None):
    n = [len(scalars), len(ins), len(raw), len(outs), len(raw_outs), len(small), len(ins), len(outs), len(scratch)]
    n += [len(ins), len(outs)]

    def kernel(*refs):
        groups = []
        at = 0
        for count in n:
            groups.append(refs[at : at + count])
            at += count
        sc, hi, hr, ho, hro, sm, vi, vo, ex, si, so = groups
        stage = Stage(list(zip(hi, vi)), si, list(zip(ho, vo)), so)
        body(stage, sc, vi, hr, vo, hro, sm, ex)
        stage.done()

    held = [pltpu.VMEM(a.shape, a.dtype) for a, _ in ins] + [pltpu.VMEM(shape, dtype) for shape, dtype, _ in outs]
    size = sum(a.size * a.dtype.itemsize for a, _ in ins)
    for shape, dtype, _ in outs:
        count = jnp.dtype(dtype).itemsize
        for extent in shape:
            count *= extent
        size += count
    for one in scratch:
        if jnp.issubdtype(one.dtype, jnp.floating):
            count = jnp.dtype(one.dtype).itemsize
            for extent in one.shape:
                count *= extent
            size += count
    got = kernel_call(
        kernel,
        us,
        size // 2**20 + 12,
        smem() * len(scalars) + hbm(len(ins) + len(raw)),
        hbm(len(outs) + len(raw_outs)) + vmem(len(small)),
        [shaped(shape, dtype) for shape, dtype, _ in outs] + list(raw_outs) + list(small),
        held + list(scratch) + [sems(k) for _, k in ins] + [sems(k) for _, _, k in outs],
        aliases or {},
    )(*scalars, *[a for a, _ in ins], *raw)
    return got[0] if single else got


def sems(count):
    return pltpu.SemaphoreType.DMA((count,))


def next_rows(stage, x, a, b, bias, x_out, n_out):
    keep = keep_of(x.shape[1])
    rows = x.shape[0] // 4
    stage.need(3)
    for part in range(4):
        stage.need(0, 1, 2, part=part)
        for start in range(part * rows, part * rows + rows, 128):
            at = pl.ds(start, 128)
            value = x[at, :] + (a[at, :].astype(f32) + b[at, :].astype(f32) + bias[...]) * keep
            x_out[at, :] = value
            _, factor = norm_of(value)
            n_out[at, :] = (value * factor).astype(bf16)
        stage.push(0, 1, part=part)


def next_stream(x, a, b, bias):
    def body(stage, scalars, ins, raw, outs, raw_outs, small, scratch):
        next_rows(stage, *ins, *outs)

    return staged(
        body, 3, [], [(x, 4), (a, 4), (b, 4), (bias[None], 1)], [], [(x.shape, f32, 4), (x.shape, bf16, 4)]
    )


def gelu_parts(x):
    a = 0.7978845608028654
    square = x * x
    s = 0.5 + 0.5 * jnp.tanh(x * (a + (a * 0.044715) * square))
    value = x * s
    slope = s + (value - value * s) * (2 * a + (6 * a * 0.044715) * square)
    return value.astype(bf16), slope.astype(bf16)


class Units:
    def __init__(self, buffers, blocks, turned):
        self.buffers, self.blocks, self.turned = buffers, blocks, turned

    def spot(self, where, step, column):
        if not self.turned:
            return step, column
        return jnp.bitwise_xor(where[2], step), jnp.bitwise_xor(where[0], column)

    def copies(self, refs, where, first, target, sem):
        count = target.shape[2]
        copies = [[], [], [], []]
        for i, (step, column, buffer, index) in enumerate(self.blocks):
            source = refs[buffer].at[index + (pl.ds(first, count),)]
            chip, spot = self.spot(where, step, column)
            copies[step].append(pltpu.make_async_copy(source, target.at[chip, spot], sem.at[i]))
        return copies


def turned_units(pieces):
    blocks = []
    for buffer, (array, column, chip) in enumerate(pieces):
        blocks += [(chip + i, column, buffer, (i,)) for i in range(array.shape[0])]
    return Units([place[0] for place in pieces], blocks, True)


def plain_units(array):
    return Units([array], [(chip, column, 0, (column, chip)) for chip in range(4) for column in range(4)], False)


def column_of(row):
    return jnp.broadcast_to(row, (8, row.shape[1])).T[:, 0:1]


def row_of(column):
    return jnp.broadcast_to(column, (column.shape[0], 128)).T[0:1, :]


def mlp_forward(where, x, a, b, bias, units, step, b_up):
    tokens, width = x.shape
    part = 4 * step

    def body(stage, scalars, ins, raw, outs, raw_outs, small, scratch):
        up, down, up_sem, down_sem = scratch
        x1, n1, g, slope, out = outs
        up_copies = units.copies(raw, scalars[0], 0, up, up_sem)
        down_copies = units.copies(raw, scalars[0], step, down, down_sem)
        for copies in up_copies + down_copies:
            run(copies, "start")
        next_rows(stage, *ins[:4], x1, n1)
        stage.need(4)
        for copies in up_copies:
            run(copies, "wait")
        for t in range(4):
            chip, _ = units.spot(scalars[0], t, 0)
            rows = pl.ds(pl.multiple_of(chip * part, part), part)
            h = dot_nt(up[chip].reshape(part, width), n1[...]) + column_of(ins[4][:, rows])
            g[rows, :], slope[rows, :] = gelu_parts(h)
        stage.push(2, 3)
        for copies in down_copies:
            run(copies, "wait")
        for i, first in enumerate(range(0, width, 256)):
            columns = pl.ds(first, 256)
            out[:, columns] = dot_tn(g[...], down[:, :, :, columns].reshape(4 * part, 256)).astype(bf16)
        stage.push(4)

    hidden = 4 * part
    return staged(
        body,
        14,
        [where],
        [(x, 4), (a, 4), (b, 4), (bias[None], 1), (b_up[None], 1)],
        units.buffers,
        [
            (x.shape, f32, 4),
            (x.shape, bf16, 4),
            ((hidden, tokens), bf16, 1),
            ((hidden, tokens), bf16, 1),
            (x.shape, bf16, 1),
        ],
        scratch=[pltpu.VMEM((4, 4, step, width), bf16)] * 2 + [sems(16)] * 2,
    )


def mlp_backward(where, before, n1, g, slope, units, step):
    first = len(before) == 2
    tokens, width = n1.shape
    part = 4 * step
    hidden = 4 * part

    def body(stage, scalars, ins, raw, outs, raw_outs, small, scratch):
        up, down, dm, dh, gw, up_sem, down_sem, gw_sem = scratch
        dx_out, dn_out = outs
        place = scalars[0]
        count = len(before)
        n1_in, s_in, g_in = ins[count:]
        down_copies = units.copies(raw, place, step, down, down_sem)
        up_copies = units.copies(raw, place, 0, up, up_sem)
        for copies in down_copies + up_copies:
            run(copies, "start")
        keep = keep_of(width)
        total = jnp.zeros((1, width), f32)
        rows = tokens // 4
        for k in range(4):
            for start in range(k * rows, k * rows + rows, 128):
                if first:
                    stage.need(k // 2, part=k)
                    at = (k % 2) * rows + start - k * rows
                    core = place[1] if k < 2 else 1 - place[1]
                    dx = ins[k // 2][pl.ds(at, 128), :].astype(f32)
                    spot = pl.ds(pl.multiple_of(core * (tokens // 2) + at, 128), 128)
                else:
                    stage.need(0, 1, 2, 3, part=k)
                    spot = pl.ds(start, 128)
                    dn = ins[2][spot, :].astype(f32) + ins[3][spot, :].astype(f32)
                    dx = ins[0][spot, :] + norm_back(ins[1][spot, :], dn)
                dx_out[spot, :] = dx
                low = (dx * keep).astype(bf16)
                dm[spot, :] = low
                total = total + jnp.sum(low.astype(f32), axis=0, keepdims=True)
        stage.push(0)
        bu_ref, bd_ref = small
        bd_ref[...] = jnp.broadcast_to(total, bd_ref.shape)
        stage.need(count, count + 1, count + 2)
        for copies in down_copies:
            run(copies, "wait")
        stores = []
        for t in range(4):
            chip, _ = units.spot(place, t, 0)
            at = pl.ds(pl.multiple_of(chip * part, part), part)
            d_hidden = dot_nt(down[chip].reshape(part, width), dm[...]) * s_in[at, :].astype(f32)
            bu_ref[:, at] = jnp.broadcast_to(row_of(jnp.sum(d_hidden, axis=1, keepdims=True)), (8, part))
            d_hidden = d_hidden.astype(bf16)
            dh[at, :] = d_hidden
            gw[t, :, 0:step, :] = dot_nn(d_hidden, n1_in[...]).astype(bf16).reshape(4, step, width)
            gw[t, :, step:, :] = dot_nn(g_in[at, :], dm[...]).astype(bf16).reshape(4, step, width)
            for j in range(4):
                if units.turned:
                    near, far, kept = raw_outs
                    target = {
                        (2, 0): near.at[0], (3, 0): near.at[1], (1, 1): far.at[0], (3, 1): far.at[1],
                        (0, 0): kept.at[0], (1, 0): kept.at[1], (0, 1): kept.at[2], (2, 1): kept.at[3],
                    }[(j, t // 2)].at[t % 2]
                    source = gw.at[t, jnp.bitwise_xor(place[0], j)]
                else:
                    target = raw_outs[0].at[j, t]
                    source = gw.at[t, j]
                stores.append(pltpu.make_async_copy(source, target, gw_sem.at[4 * t + j]))
        run(stores, "start")
        stage.pushed.extend(stores)
        for copies in up_copies:
            run(copies, "wait")
        for first_column in range(0, width, 256):
            columns = pl.ds(first_column, 256)
            dn_out[:, columns] = dot_tn(dh[...], up[:, :, :, columns].reshape(hidden, 256)).astype(bf16)
        stage.push(1)

    ins = [(a, 2) for a in before] if first else [(a, 4) for a in before]
    if units.turned:
        raw_outs = [shaped((2, 2, 2 * step, width), bf16)] * 2 + [shaped((4, 2, 2 * step, width), bf16)]
    else:
        raw_outs = [shaped((4, 4, 2 * step, width), bf16)]
    return staged(
        body,
        18,
        [where],
        ins + [(n1, 1), (slope, 1), (g, 1)],
        units.buffers,
        [((tokens, width), f32, 1), ((tokens, width), bf16, 1)],
        raw_outs,
        [shaped((8, hidden), f32), shaped((8, width), f32)],
        [pltpu.VMEM((4, 4, step, width), bf16)] * 2
        + [pltpu.VMEM((tokens, width), bf16), pltpu.VMEM((hidden, tokens), bf16)]
        + [pltpu.VMEM((4, 4, 2 * step, width), bf16)]
        + [sems(16)] * 3,
    )


def out_backward(dx, x, a, b, rows):
    tokens, width = dx.shape
    heads = rows.shape[0]

    def body(stage, scalars, ins, raw, outs, raw_outs, small, scratch):
        w_ref, w_sem = scratch
        load = pltpu.make_async_copy(raw[0], w_ref, w_sem.at[0])
        load.start()
        dx1, da_out, do = outs
        keep = keep_of(width)
        total = jnp.zeros((1, width), f32)
        load.wait()
        for k in range(4):
            stage.need(0, 1, 2, 3, part=k)
            for start in (0, 128):
                at = pl.ds(k * 256 + start, 128)
                dn = ins[2][at, :].astype(f32) + ins[3][at, :].astype(f32)
                value = ins[0][at, :] + norm_back(ins[1][at, :], dn)
                dx1[at, :] = value
                da = (value * keep).astype(bf16)
                da_out[at, :] = da
                total = total + jnp.sum(da.astype(f32), axis=0, keepdims=True)
            at = pl.ds(k * 256, 256)
            do[at, :] = dot_nt(da_out[at, :], w_ref[...]).astype(bf16)
            stage.push(0, 1, 2, part=k)
        small[0][...] = jnp.broadcast_to(total, small[0].shape)

    return staged(
        body,
        5,
        [],
        [(dx, 4), (x, 4), (a, 4), (b, 4)],
        [rows],
        [((tokens, width), f32, 4), ((tokens, width), bf16, 4), ((tokens, heads), bf16, 4)],
        small=[shaped((8, width), f32)],
        scratch=[pltpu.VMEM((heads, width), bf16), sems(1)],
    )


def piece_copies(where, pieces, rows, held, sem):
    copies = []
    for i in range(4):
        for j in (0, 1):
            if len(pieces) > 1:
                spot = 2 * jnp.bitwise_xor(where[0], i) + jnp.bitwise_xor(where[1], j)
                source = pieces[4 * j + i]
            else:
                spot = 2 * i + j
                source = pieces[0].at[spot]
            copies.append(
                pltpu.make_async_copy(source.at[pl.ds(0, rows)], held.at[spot], sem.at[2 * i + j])
            )
    return copies


def units_out(where, layer, layers, pieces, step, before):
    width = pieces[0].shape[-1]
    hidden = 8 * step
    count = len(pieces)

    def body(stage, scalars, ins, raw, outs, raw_outs, small, scratch):
        held, up, down, in_sem, out_sem = scratch
        copies = piece_copies(scalars[0], raw[:count], 2 * step, held, in_sem)
        run(copies, "start")
        run(copies, "wait")
        for i in range(8):
            down[pl.ds(i * step, step), :] = held[i, step:, :].astype(f32)
        store = pltpu.make_async_copy(down, raw_outs[1].at[layer], out_sem.at[0])
        store.start()
        up[...] = held[:, :step, :].reshape(hidden, width).astype(f32).T
        last = pltpu.make_async_copy(up, raw_outs[0].at[layer], out_sem.at[1])
        last.start()
        run([store, last], "wait")

    return staged(
        body,
        5,
        [where],
        [],
        list(pieces) + list(before),
        [],
        [shaped((layers, width, hidden), f32), shaped((layers, hidden, width), f32)],
        (),
        [
            pltpu.VMEM((8, 2 * step, width), bf16),
            pltpu.VMEM((width, hidden), f32),
            pltpu.VMEM((hidden, width), f32),
            sems(8),
            sems(2),
        ],
        aliases={1 + count: 0, 2 + count: 1} if before else {},
    )


def heads_out(where, layer, layers, pieces, part, before):
    rows, width = pieces[0].shape[-2:]
    local = 8 * part
    count = len(pieces)

    def body(stage, scalars, ins, raw, outs, raw_outs, small, scratch):
        held, value, in_sem, out_sem = scratch
        copies = piece_copies(scalars[0], raw[:count], rows, held, in_sem)
        run(copies, "start")
        run(copies, "wait")
        stores = []
        for kind in range(4):
            value[kind] = held[:, kind * part : (kind + 1) * part, :].astype(f32).reshape(local, width)
            target = raw_outs[0].at[layer, kind] if kind < 3 else raw_outs[1].at[layer]
            stores.append(pltpu.make_async_copy(value.at[kind], target, out_sem.at[kind]))
            stores[-1].start()
        small[0][...] = jnp.sum(held[:, rows - 8 :, :].astype(f32), axis=0)
        run(stores, "wait")

    return staged(
        body,
        3,
        [where],
        [],
        list(pieces) + list(before),
        [],
        [shaped((layers, 3, local, width), f32), shaped((layers, local, width), f32)],
        [shaped((8, width), f32)],
        [pltpu.VMEM((8, rows, width), bf16), pltpu.VMEM((4, local, width), f32), sems(8), sems(4)],
        aliases={1 + count: 0, 2 + count: 1} if before else {},
    )


def heads_copies(kinds, part, s_ref, refs, turned, outs, sem):
    copies = []
    for kind in range(kinds):
        if turned:
            rows = pl.ds(kind * part, part)
            sources = [(refs[j].at[pl.ds(2 * h, 2), rows], j, h) for j in range(3) for h in (0, 1)]
            sources += [(refs[3].at[:, rows], 3, 0), (refs[4].at[:, rows], 3, 1)]
        else:
            first = refs[0].shape[2] - kinds * part
            pair = pl.ds(2 * s_ref[1], 2)
            sources = [(refs[0].at[j, pair, pl.ds(first + kind * part, part)], j, 0) for j in range(4)]
            sources += [(refs[1].at[j, :, pl.ds(kind * part, part)], j, 1) for j in range(4)]
        out = outs[0].at[kind] if kind < kinds - 1 else outs[1].at[0]
        for i, (source, j, h) in enumerate(sources):
            column = jnp.bitwise_xor(s_ref[0], j) if turned else j
            spot = 2 * column + jnp.bitwise_xor(s_ref[1], h)
            copies.append(pltpu.make_async_copy(source, out.at[pl.ds(0, 2), spot], sem.at[kind * 8 + i]))
    return copies


def heads_rows(refs, where, kinds, part, turned):
    width = refs[0].shape[-1]

    def body(stage, scalars, ins, raw, outs, raw_outs, small, scratch):
        copies = heads_copies(kinds, part, scalars[0], raw, turned, outs, scratch[0])
        run(copies, "start")
        for kind in range(kinds):
            run(copies[8 * kind : 8 * kind + 8], "wait")
            if kind < kinds - 1:
                stage.push(0, part=kind)
            else:
                stage.push(1)

    got = staged(
        body,
        3,
        [where],
        [],
        refs,
        [((kinds - 1, 2, 8, part, width), bf16, kinds - 1), ((1, 2, 8, part, width), bf16, 1)],
        scratch=[sems(8 * kinds)],
    )
    return [value.reshape(-1, width) for value in got]


def heads_terms(where, dq, dk, dv, o, dkr, dvr, n, far_mine, far_other, da, part, turned):
    tokens, width = n.shape
    quarter = tokens // 2

    def body(stage, scalars, ins, raw, outs, raw_outs, small, scratch):
        value_ref, sem = scratch
        s_ref = scalars[0]
        mine = pl.ds(pl.multiple_of(s_ref[1] * quarter, quarter), quarter)
        other = pl.ds(pl.multiple_of((1 - s_ref[1]) * quarter, quarter), quarter)

        def near(i, y):
            stage.need(i, y)
            return dot_tn(ins[i][...], ins[y][...])

        def far(i):
            stage.need(i, 7, 8)
            return dot_tn(ins[i][mine, :], ins[7][...]) + dot_tn(ins[i][other, :], ins[8][...])

        terms = (lambda: near(0, 6), lambda: near(1, 6) + far(4), lambda: near(2, 6) + far(5), lambda: near(3, 9))
        for kind, term in enumerate(terms):
            value_ref[kind] = term().astype(bf16).reshape(2, 8, part, width)
            rows = pl.ds(kind * part, part)
            for j in range(4):
                for mine_too in (0, 1):
                    if turned:
                        target = raw_outs[j].at[pl.ds(2 * (1 - mine_too), 2), rows]
                        column = jnp.bitwise_xor(s_ref[0], j)
                    else:
                        target, column = raw_outs[1 - mine_too].at[j, :, rows], j
                    spot = 2 * column + (s_ref[1] if mine_too else 1 - s_ref[1])
                    copy = pltpu.make_async_copy(
                        value_ref.at[kind, :, spot], target, sem.at[kind * 8 + 2 * j + mine_too]
                    )
                    copy.start()
                    stage.pushed.append(copy)

    ins = [dq, dk, dv, o, dkr, dvr, n, far_mine, far_other, da]
    if turned:
        raw_outs = [shaped((4, 4 * part, width), bf16)] * 4
    else:
        raw_outs = [shaped((4, 2, 4 * part, width), bf16)] * 2
    return staged(
        body,
        6,
        [where],
        [(a, 1) for a in ins],
        [],
        [],
        raw_outs,
        scratch=[pltpu.VMEM((4, 2, 8, part, width), bf16), sems(32)],
    )


def far_project(where, mine, other, rows, offset):
    quarter, width = mine.shape
    heads = rows.shape[0] // 3

    def body(stage, scalars, ins, raw, outs, raw_outs, small, scratch):
        w_ref, w_sem = scratch
        load = pltpu.make_async_copy(raw[0].at[pl.ds(heads, 2 * heads)], w_ref, w_sem.at[0])
        load.start()
        stage.need(2)
        load.wait()
        for i in (0, 1):
            stage.need(i)
            core = scalars[0][1] if i == 0 else 1 - scalars[0][1]
            at = pl.ds(pl.multiple_of(core * quarter, quarter), quarter)
            outs[0][at, :] = (dot_nt(ins[i][...], w_ref[...]) + ins[2][...]).astype(bf16)
        stage.push(0)

    return staged(
        body,
        2,
        [where],
        [(mine, 1), (other, 1), (offset[None], 1)],
        [rows],
        [((2 * quarter, 2 * heads), bf16, 1)],
        scratch=[pltpu.VMEM((2 * heads, width), bf16), sems(1)],
        single=True,
    )


def far_terms(where, dkr, dvr, rows):
    quarter, width = dkr.shape[0] // 2, rows.shape[1]
    heads = dkr.shape[1]

    def body(stage, scalars, ins, raw, outs, raw_outs, small, scratch):
        w_ref, w_sem = scratch
        load = pltpu.make_async_copy(raw[0].at[pl.ds(heads, 2 * heads)], w_ref, w_sem.at[0])
        load.start()
        stage.need(0, 1)
        load.wait()
        for i, core in enumerate((1 - scalars[0][1], scalars[0][1])):
            at = pl.ds(pl.multiple_of(core * quarter, quarter), quarter)
            value = dot_nn(ins[0][at, :], w_ref[pl.ds(0, heads), :])
            outs[i][...] = (value + dot_nn(ins[1][at, :], w_ref[pl.ds(heads, heads), :])).astype(bf16)
            stage.push(i)

    return staged(
        body,
        2,
        [where],
        [(dkr, 1), (dvr, 1)],
        [rows],
        [((quarter, width), bf16, 1)] * 2,
        scratch=[pltpu.VMEM((2 * heads, width), bf16), sems(1)],
    )


def near_terms(where, dq, dk, dv, back, rows):
    tokens, heads = dq.shape
    width = rows.shape[1]
    quarter = tokens // 2

    def body(stage, scalars, ins, raw, outs, raw_outs, small, scratch):
        w_ref, w_sem = scratch
        load = pltpu.make_async_copy(raw[0].at[pl.ds(0, 3 * heads)], w_ref, w_sem.at[0])
        load.start()
        stage.need(0, 1, 2, 3)
        load.wait()
        for core in (0, 1):
            at = pl.ds(core * quarter, quarter)
            value = ins[3][...].astype(f32) * jnp.where(scalars[0][1] == core, 1.0, 0.0)
            for i in range(3):
                value = value + dot_nn(ins[i][at, :], w_ref[pl.ds(i * heads, heads), :])
            outs[0][at, :] = value.astype(bf16)
            stage.push(0, part=core)

    return staged(
        body,
        3,
        [where],
        [(dq, 1), (dk, 1), (dv, 1), (back, 1)],
        [rows],
        [((tokens, width), bf16, 2)],
        scratch=[pltpu.VMEM((3 * heads, width), bf16), sems(1)],
        single=True,
    )


def hold(value, *marks):
    return value if not marks else lax.optimization_barrier((value,) + marks)[0]


class Moves:
    def __init__(self, groups, pieces, chips):
        self.sizes = (groups, pieces, 2, chips)
        self.p = lax.axis_index("p")
        self.c = lax.axis_index("c")
        self.z = lax.axis_index("mp")
        self.spot = 2 * (self.z % 2) + self.c

    def permute(self, value, target):
        groups, pieces, cores, chips = self.sizes
        place = lambda g, p, c, z: ((g * pieces + p) * cores + c) * chips + z
        pairs = [
            (place(g, p, c, z), place(*target(g, p, c, z)))
            for g in range(groups)
            for p in range(pieces)
            for c in range(cores)
            for z in range(chips)
        ]
        return lax.ppermute(value, AXES, pairs)

    def core(self, value):
        return self.permute(value, lambda g, p, c, z: (g, p, 1 - c, z))

    def chip(self, value, bit):
        return self.permute(value, lambda g, p, c, z: (g, p, c, z ^ bit))

    def column(self, value, bit):
        return self.permute(value, lambda g, p, c, z: (g, p ^ bit, c, z))

    def in_order(self, mine, other):
        return jnp.where(self.c == 0, jnp.concatenate([mine, other]), jnp.concatenate([other, mine]))

    @staticmethod
    def shuffle(blocks, index):
        odd = (index % 2) == 1
        high = index >= 2
        blocks = [jnp.where(odd, blocks[j ^ 1], blocks[j]) for j in range(4)]
        return [jnp.where(high, blocks[j ^ 2], blocks[j]) for j in range(4)]

    def to_rows(self, block, mark=None, tie=None):
        quarter = block.shape[0] // 4
        got, sends = [], []
        for k in range(4):
            spot = self.z ^ k
            which = jnp.where(spot == 0, 0, jnp.where(spot == 1, 3, spot - 1))
            if mark is not None:
                which = which + jnp.isnan(mark[0, 0]).astype(jnp.int32)
            sends.append(lax.dynamic_slice_in_dim(block, which * quarter, quarter, 0).astype(bf16))
        tied = None if tie is None else hold(tie, *sends)
        for k in range(4):

            def target(g, p, c, z, k=k):
                t = z ^ k
                return (g, p, t % 2, 2 * c + t // 2)

            got.append(self.permute(sends[k], target))
        return got if tie is None else (got, tied)

    def column_blocks(self, rows):
        width = rows[0].shape[1] // 4
        sends = []
        for value in rows:
            blocks = [value[:, j * width : (j + 1) * width].astype(bf16) for j in range(4)]
            sends.append(self.shuffle(blocks, self.spot))
        return [jnp.stack([send[k] for send in sends]) for k in range(4)]

    def to_columns(self, sends):
        got = []
        for k in range(4):

            def target(g, p, c, z, k=k):
                t = 2 * (z % 2) + c
                return (g, p, z // 2, t ^ k)

            got.append(self.permute(sends[k], target))
        return got

    def whole_columns(self, got):
        parts = self.shuffle(got, self.z)
        whole = jnp.concatenate([parts[0], parts[2], parts[3], parts[1]], axis=1).astype(f32)
        return [whole[i] for i in range(whole.shape[0])]


class Columns:
    def __init__(self, mv, rows):
        width = rows.shape[1] // 4
        self.mv = mv
        self.blocks = mv.shuffle([rows[:, j * width : (j + 1) * width].astype(bf16) for j in range(4)], mv.z)
        self.first = mv.chip(jnp.stack([self.blocks[1], self.blocks[3]]), 1)

    def two(self, *marks):
        second = hold(jnp.stack([self.blocks[2], self.first[1]]), *marks)
        self.second = self.mv.chip(second, 2)

    def finish(self, *marks):
        mv = self.mv
        own = jnp.stack([self.blocks[0], self.first[0]])
        home = mv.c == mv.z // 2
        stay, leave = jnp.where(home, own, self.second), jnp.where(home, self.second, own)
        third = mv.core(hold(leave, *marks))
        every = jnp.stack([stay, third]).reshape((4,) + own.shape[1:])
        spots = [2 * (core ^ mv.c) + (half ^ (mv.z % 2)) for half, core in ((0, 0), (1, 0), (1, 1), (0, 1))]
        whole = [lax.dynamic_index_in_dim(every, spot, 0, keepdims=False) for spot in spots]
        return jnp.concatenate(whole).astype(f32)


class Gather:
    def __init__(self, mv, piece):
        self.mv, self.piece = mv, piece
        self.one = mv.chip(piece, 1)
        self.three = mv.chip(piece, 3)

    def second(self, *marks):
        self.two = self.mv.chip(hold(self.three, *marks), 1)

    def chips(self):
        return jnp.stack([self.piece, self.one, self.two, self.three])

    def heads(self, rows):
        every = self.chips()[:, :rows].reshape((2, 2, rows) + self.piece.shape[1:])
        got = self.mv.core(lax.dynamic_index_in_dim(every, 1 - self.mv.c, 0, keepdims=False))
        own = lax.dynamic_index_in_dim(every, self.mv.c, 0, keepdims=False)
        return jnp.concatenate([own, got])


class Across:
    def __init__(self, mv, group, chip=0):
        self.mv, self.group, self.chip = mv, group, chip
        self.x = mv.column(group, 1)
        self.y = mv.column(group, 2)

    def corner(self, *marks):
        half = self.group.shape[0] // 2
        x, y = hold((self.x, self.y), *marks)
        self.low_send, self.high_send = x[:half], y[half:]
        return self.low_send, self.high_send

    def finish(self):
        half = self.group.shape[0] // 2
        low = self.mv.column(self.low_send, 2)
        high = self.mv.column(self.high_send, 1)
        chip = self.chip
        return [(self.group, 0, chip), (self.x, 1, chip), (self.y, 2, chip), (low, 3, chip), (high, 3, chip + half)]


def add(*terms):
    return sum(t.astype(f32) for t in terms).astype(bf16)


class Scatter:
    def __init__(self, mv, near, far, kept):
        self.mv, self.kept = mv, kept
        self.near_y = mv.column(near, 2)
        self.far_x = mv.column(far, 1)

    def two(self, *marks):
        self.near_y, self.far_x = hold((self.near_y, self.far_x), *marks)
        self.near_send = add(self.kept[1], self.near_y[1])
        self.far_send = add(self.kept[3], self.far_x[1])
        return self.near_send, self.far_send

    def three(self, *marks):
        near_x = self.mv.column(self.near_send, 1)
        far_y = self.mv.column(self.far_send, 2)
        self.near_x, self.far_y = hold((near_x, far_y), *marks)
        return self.near_x, self.far_y

    def chips(self):
        near = add(self.kept[0], self.near_y[0], self.near_x)
        far = add(self.kept[2], self.far_x[0], self.far_y)
        return [near[0], near[1], far[0], far[1]]


def sum_columns(mv, terms, *marks):
    got = [mv.column(terms[j], j) for j in (1, 2, 3)]
    return add(terms[0], *hold(got, *marks))


def sum_chips(mv, terms, *marks):
    got = [mv.chip(terms[s], s) for s in (1, 2, 3)]
    return add(terms[0], *hold(got, *marks))


def all_columns(mv, mine, *marks):
    four = [mine] + [mv.column(mine, j) for j in (1, 2, 3)]
    return four + [mv.core(hold(value, *marks)) for value in four]


def per_device(stream, seq_lens, w_qkv, b_qv, w_out, b_out, w_up, b_up, w_down, b_down, cotangent):
    groups = lax.axis_size("g")
    mv = Moves(groups, lax.axis_size("p"), lax.axis_size("mp"))
    p, c, z = mv.p, mv.c, mv.z
    length, local = stream.shape
    chips = lax.axis_size("mp")
    width = local * chips
    layers = w_qkv.shape[0]
    hidden = w_up.shape[2]
    size = width // HEADS
    quarter = length // 4
    tokens = 2 * quarter
    half_heads = 2 * local
    att = Attention(tokens, HEADS // 2, size)
    keep = (jnp.arange(width, dtype=jnp.int32) < width - 1).astype(f32)[None, :]
    step = hidden // (2 * PIECES)
    part = local // (2 * PIECES)
    every = range(layers)
    where = jnp.stack([p, c, z]).astype(jnp.int32)
    core = c.astype(jnp.int32)

    def spot_of(mark):
        spot = 2 * p + c
        return spot if mark is None else spot + jnp.isnan(mark[0, 0]).astype(jnp.int32)

    def head_piece(layer, mark=None):
        spot = spot_of(mark)
        cut = lax.dynamic_slice_in_dim(w_qkv[layer], spot * part, part, 2)
        cut = jnp.transpose(cut, (1, 2, 0)).reshape(3 * part, width)
        return jnp.concatenate([cut, lax.dynamic_slice_in_dim(w_out[layer], spot * part, part, 0)])

    def unit_piece(layer, mark=None):
        spot = spot_of(mark)
        up = lax.dynamic_slice_in_dim(w_up[layer], spot * step, step, 1).T
        return jnp.concatenate([up, lax.dynamic_slice_in_dim(w_down[layer], spot * step, step, 0)])

    flat = jnp.concatenate([b_qv.reshape(-1), b_out.reshape(-1), b_up.reshape(-1), b_down.reshape(-1)])
    flat = flat.reshape(-1, width)
    high = flat.astype(bf16)
    low = (flat - high.astype(f32)).astype(bf16)
    heads = Gather(mv, jnp.concatenate([head_piece(0), high, low]))

    blocks = mv.to_rows(stream)
    heads.second()
    gathered = heads.chips()
    biases = gathered[:, 4 * part :].astype(f32).reshape(chips, 2, -1)
    biases = biases[:, 0] + biases[:, 1]
    heads = Across(mv, heads.heads(4 * part))
    x_mine, n_mine = quarter_rows(hold(blocks, heads.group), mv.spot, True)
    n_far = mv.chip(n_mine, 1)
    x, n = both_rows(hold(x_mine, *heads.corner()), mv.core(x_mine), core)
    biases = jnp.concatenate([lax.dynamic_index_in_dim(biases, z ^ i, 0) for i in range(4)])
    lens = jnp.where(c == z // 2, seq_lens, mv.core(seq_lens))
    flags = jnp.stack([(lens[0] > quarter).astype(jnp.int32), 1 - z % 2])
    units = Gather(mv, unit_piece(0, x))
    arrays = [place[0] for place in heads.finish()]
    arrays, n_far = hold((arrays, n_far), x)
    arrays = hold(arrays, n_far)
    head_rows = {0: heads_rows(arrays, where, 4, part, True)}

    cuts = [0, layers * 2 * local, layers * local, layers * hidden, layers * local]
    ends = [sum(cuts[: i + 1]) for i in range(5)]

    def bias(i, shape):
        return biases[:, ends[i] : ends[i + 1]].reshape((chips,) + shape)

    def bias_qv(layer):
        every_chip = bias(0, (layers, 2, local))[:, layer]
        pair = [2 * c, 2 * c + 1]
        if layer == 0:
            pair = [z ^ i for i in pair]
        two = jnp.stack([lax.dynamic_index_in_dim(every_chip, i, 0, keepdims=False) for i in pair], axis=1)
        return two.reshape(2, half_heads)

    def wide(i):
        return jnp.transpose(bias(i, (layers, local)), (1, 0, 2)).reshape(layers, width)

    bias_out, bias_down = wide(1), wide(3)
    all_up = lax.dynamic_index_in_dim(bias(2, (layers, PIECES, 2, step)), c, 3, keepdims=False)
    bias_up = jnp.transpose(all_up, (1, 0, 2, 3)).reshape(layers, chips * PIECES * step)

    saved = []
    outs = []
    pieces = {}
    scale = float(size) ** -0.5
    zero = jnp.zeros((half_heads,), f32)
    mult = jnp.concatenate([zero + scale, zero + 1.0, zero + 1.0])
    for layer in every:
        last = layer + 1 == layers
        rows, out_rows = head_rows[layer]
        pair = bias_qv(layer)
        offset = jnp.concatenate([pair[0], zero, pair[1]])
        proj = dot_nt(hold(n, units.three) if layer == 0 else n, rows)
        qkv = ((proj + offset).astype(bf16).astype(f32) * mult).astype(bf16)
        local_in = qkv
        if layer == 0:
            units.second(rows)
            group = hold(units.chips(), qkv)
            local_in, n_far = hold((qkv, n_far), group)
            local_in = hold(local_in, n_far)
            units = Across(mv, group)
        if last:
            cot_blocks, local_in = mv.to_rows(cotangent, n, local_in)
        acc, high, sums = att.forward_local(flags, local_in)
        if not last:
            piece = jnp.concatenate([unit_piece(layer + 1, n_mine), head_piece(layer + 1, n_mine)])
            piece = hold(piece, units.group) if layer == 0 else piece
            piece = hold(lax.all_gather(piece, "mp", axis=0), acc)
            more_heads = lax.all_gather(piece[:, 2 * step :], "p", axis=0)
            more_units = lax.all_gather(piece[:, : 2 * step], "p", axis=0)
        n_far = hold(n_far, acc)
        n_far_other = mv.core(n_far)
        kv = far_project(where, n_far, n_far_other, rows, offset[half_heads:])
        kv_in = kv
        if layer == 0:
            kv_in = hold(kv_in, units.corner(acc))
            finished = units.finish()
            pieces[0] = turned_units(finished)
        o, lse = att.forward_remote(flags, qkv, kv_in, acc, high, sums)
        out_in = hold(o, *finished) if layer == 0 else o
        out_in = hold(out_in, *cot_blocks) if last else out_in
        branch = dot_nn(out_in, out_rows).astype(bf16)
        branch_in = branch
        if layer == 1:
            sends = mv.column_blocks([outs[0]])
            branch_in = hold(branch, *sends)
            first_blocks = mv.to_columns(sends)
        x1, n1, g, slope, branch_two = mlp_forward(
            where, x, branch_in, mv.core(branch), bias_out[layer], pieces[layer], step, bias_up[layer]
        )
        if layer == 1:
            branch_two = hold(branch_two, *first_blocks)
        saved.append((x, n, n_far, n_far_other, qkv, kv, o, lse, x1, n1, g, slope))
        if not last:
            pieces[layer + 1] = plain_units(more_units)
            more_heads = hold(more_heads, branch_two)
            got = mv.core(lax.dynamic_slice_in_dim(more_heads, 2 * (1 - c), 2, 1))
            head_rows[layer + 1] = heads_rows([more_heads, got], where, 4, part, False)
        x, n = next_stream(x1, branch_two, mv.core(branch_two), bias_down[layer])
        if not last:
            n_far = mv.chip(lax.dynamic_slice_in_dim(n, c * quarter, quarter, 0), 1)
        if layer == 0 or last:
            outs.append(lax.dynamic_slice_in_dim(x, c * quarter, quarter, 0))

    def all_groups(value):
        return lax.psum(value, "g") if groups > 1 else value

    gb_q, gb_v, gb_out, gb_up, gb_down = {}, {}, {}, {}, {}
    unit_grads, head_grads = [], []

    def everywhere(mine, fast, *marks):
        mine = all_groups(mine)
        return all_columns(mv, mine, *marks) if fast else [lax.all_gather(mine, ("p", "c"), axis=0)]

    def end_units(layer, mine, fast, *marks):
        unit_grads[:] = units_out(where, layer, layers, everywhere(mine, fast, *marks), step, unit_grads)

    def end_heads(layer, mine, fast):
        got = heads_out(where, layer, layers, everywhere(mine, fast), part, head_grads)
        head_grads[:] = got[:2]
        return got[2]

    def summed(terms):
        return lax.psum_scatter(terms, "p", scatter_dimension=0)

    def summed_chips(mine):
        return lax.psum_scatter(mine, "mp", scatter_dimension=0)

    (cot_mine,) = quarter_rows(cot_blocks, mv.spot, False)
    def bias_rows():
        once = (c == 0).astype(f32)

        def by_chip(values):
            rows = jnp.stack([values[i][0] for i in every]).reshape(layers, chips, local) * once
            return jnp.transpose(rows, (1, 0, 2)).reshape(chips, -1)

        def own_chips(layer):
            two = jnp.stack([gb_q[layer], gb_v[layer]]).reshape(2, 2, local)
            rows = []
            for chip in range(chips):
                turned = (chip ^ z) if layer == 0 else chip
                value = lax.dynamic_index_in_dim(two, turned % 2, 1, keepdims=False)
                rows.append(jnp.where(turned // 2 == c, value, 0.0))
            return jnp.stack(rows)

        qv = jnp.stack([own_chips(i) for i in every], axis=1).reshape(chips, -1)
        up = jnp.stack([gb_up[i][0] for i in every]).reshape(layers, chips, PIECES, step)
        up = jnp.transpose(up, (1, 0, 2, 3))[:, :, :, None]
        none = jnp.zeros_like(up)
        up = jnp.where(c == 0, jnp.concatenate([up, none], axis=3), jnp.concatenate([none, up], axis=3))
        flat = jnp.concatenate([qv, by_chip(gb_out), up.reshape(chips, -1), by_chip(gb_down)], axis=1)
        return flat

    sends = mv.column_blocks([outs[-1]])
    before = (hold(cot_mine, *sends), mv.core(cot_mine))
    out_blocks = mv.to_columns(sends)
    later_sums = None
    for layer in reversed(every):
        x, n, n_far, n_far_other, qkv, kv, o, lse, x1, n1, g, slope = saved[layer]
        rows, out_rows = head_rows[layer]
        if layer == 0 and later_sums is not None:
            before = (hold(before[0], later_sums[1]),) + before[1:]
        got = mlp_backward(where, before, n1, g, slope, pieces[layer], step)
        dx, dn1, terms, (gb_up[layer], gb_down[layer]) = got[0], got[1], got[2:-2], got[-2:]
        if layer == 0:
            unit_sums = Scatter(mv, *terms)
        else:
            columns_sum = summed(terms[0])
        dx1, da, do, gb_out[layer] = out_backward(dx, x1, dn1, mv.core(dn1), out_rows)
        if layer == 0 and later_sums is not None:
            done = summed_chips(hold(later_sums[1], later_sums[3]))
        dqt, dkr, dvr, inner, far_sums = att.backward_remote(flags, qkv, kv, o, do, lse)
        far_send, far_keep = far_terms(where, dkr, dvr, rows)
        far_sum = add(far_keep, mv.core(far_send))
        back = mv.chip(far_sum, 1)
        local_dqt = hold(dqt, far_sum)
        if layer == 0 and later_sums is not None:
            local_dqt = hold(local_dqt, done)
        if layer == 0:
            local_dqt = hold(local_dqt, unit_sums.two(far_send))
        dq, dk, dv, near_sums = att.backward_local(flags, qkv, do, lse, inner, local_dqt)
        if layer == 0 and later_sums is not None:
            done_heads = summed_chips(hold(later_sums[2], dq))
            end_units(later_sums[0], done, False)
        gb_q[layer] = near_sums[:, 0].reshape(-1)
        gb_v[layer] = (near_sums[:, 1] + far_sums[:, 0]).reshape(-1)
        terms_in = hold(dq, *out_blocks) if layer == layers - 1 else dq
        if layer == 0:
            terms_in = hold(terms_in, back, unit_sums.three(dq))
            if later_sums is not None:
                terms_in = hold(terms_in, later_sums[2])
        terms = heads_terms(where, terms_in, dk, dv, o, dkr, dvr, n, n_far, n_far_other, da, part, layer == 0)
        if layer > 0:
            dn = near_terms(where, hold(dq, terms), dk, dv, back, rows)
            mine, got = terms[0], mv.core(hold(terms[1], dn))
            whole = jnp.where(
                c == 0, jnp.concatenate([mine, got], axis=1), jnp.concatenate([got, mine], axis=1)
            )
            later_sums = (layer, columns_sum, summed(hold(whole, columns_sum)), dq)
        else:
            head_terms = terms
            unit_mine = unit_sums.chips()
            beside = mv.chip(jnp.stack([unit_mine[1], unit_mine[2]]), 1)
            beside = hold(beside, terms)
            across = add(unit_mine[3], beside[1])
            dn = near_terms(where, hold(dq, across), dk, dv, back, rows)
            unit_last = mv.chip(across, 3)
        before = (dx1, x, dn, mv.core(dn))
    dx1, x, dn, dn_other = before
    mine = lambda value: lax.dynamic_slice_in_dim(value, c * quarter, quarter, 0)
    dx = mine(dx1) + norm_back(mine(x), mine(dn).astype(f32) + mine(dn_other).astype(f32))
    head_got = [mv.column(head_terms[j], j) for j in (1, 2, 3)]
    columns = Columns(mv, dx * keep)
    head_got = hold(head_got, columns.first, unit_last, *unit_grads)
    unit_sum = add(unit_mine[0], beside[0], hold(unit_last, head_got))
    head_sum = add(head_terms[0], *head_got)
    head_pair = head_sum[2:]
    got = mv.core(head_pair)
    pair, other = jnp.where(c == 0, head_sum[:2], got), jnp.where(c == 0, got, head_sum[:2])
    flat = bias_rows()
    extra = jnp.concatenate([flat, jnp.zeros_like(flat)], axis=1).reshape(chips, -1, width)
    extra = [lax.dynamic_index_in_dim(extra, z ^ i, 0, keepdims=False).astype(bf16) for i in range(chips)]
    terms = [jnp.concatenate(two) for two in zip((pair[0], pair[1], other[0], other[1]), extra)]
    beside = mv.chip(jnp.stack([terms[1], terms[2]]), 1)
    across = add(terms[3], beside[1])
    head_sum = add(terms[0], beside[0], mv.chip(across, 3))
    columns.two(across)
    grad_stream = columns.finish(head_sum)
    end_units(0, hold(unit_sum, across), True, head_sum)
    bias_sums = end_heads(0, head_sum, True)
    if later_sums is not None:
        end_heads(later_sums[0], hold(done_heads, head_sum), False)
    outs = [mv.whole_columns(got)[0] for got in (first_blocks, out_blocks)]

    flat = bias_sums[: ends[4] // width].reshape(-1)
    pieces = [flat[ends[i] : ends[i + 1]] for i in range(4)]
    return (
        outs[0],
        outs[1],
        grad_stream,
        jnp.transpose(head_grads[0], (0, 3, 1, 2)),
        pieces[0].reshape(layers, 2, local),
        head_grads[1],
        pieces[1].reshape(layers, local),
        unit_grads[0],
        pieces[2].reshape(layers, hidden),
        unit_grads[1],
        pieces[3].reshape(layers, local),
    )


def solution(mesh):
    rows, chips = mesh.shape["dp"], mesh.shape["mp"]
    grid = Mesh(mesh.devices.reshape(rows // (2 * PIECES), PIECES, 2, chips), AXES)
    dp = ("g", "p", "c")
    in_specs = (
        P(dp, "mp"),
        P(dp),
        P(None, None, None, "mp"),
        P(None, None, "mp"),
        P(None, "mp", None),
        P(None, "mp"),
        P(None, None, "mp"),
        P(None, "mp"),
        P(None, "mp", None),
        P(None, "mp"),
        P(dp, "mp"),
    )
    out_specs = (
        P(dp, "mp"),
        P(dp, "mp"),
        P(dp, "mp"),
        P(None, None, None, "mp"),
        P(None, None, "mp"),
        P(None, "mp", None),
        P(None, "mp"),
        P(None, None, "mp"),
        P(None, "mp"),
        P(None, "mp", None),
        P(None, "mp"),
    )
    return jax.shard_map(per_device, mesh=grid, in_specs=in_specs, out_specs=out_specs, check_vma=False)
```
